256 devices in a mesh: seq: 64 (over x, y, z_lo, core), tensor: 4 (over z_hi).
Axes of the slice: x: 4, y: 4, z: 8 (z_hi: 4, z_lo: 2; z = z_hi * 2 + z_lo), core: 2. Of those that a mesh axis runs over, the one named last changes fastest.
Arguments:
- tokens_in: bfloat16 [2, 8192, 1536], P(None, 'seq', 'tensor'), may hold values from -6 to 6
- query_weight: bfloat16 [1536, 512], P(None, 'tensor'), may hold values from -0.22963966 to 0.22963966
- key_weight: bfloat16 [1536, 512], P(None, 'tensor'), may hold values from -0.22963966 to 0.22963966
- value_weight: bfloat16 [1536, 1536], P(None, 'tensor'), may hold values from -0.15625 to 0.15625
- out_weight: bfloat16 [1536, 1536], P('tensor'), may hold values from -1.25 to 1.25
- conv_weight: bfloat16 [3, 1536, 1536], P(None, None, 'tensor'), may hold values from -0.09375 to 0.09375
- cotangent: bfloat16 [2, 8192, 1536], P(None, 'seq', 'tensor'), may hold values from -6 to 6
Outputs:
- block_out: bfloat16 [2, 8192, 1536], P(None, 'seq', 'tensor')
- conv_grad: bfloat16 [3, 1536, 1536], P(None, None, 'tensor')
- residual_grad: bfloat16 [2, 8192, 1536], P(None, 'seq', 'tensor')
The draws below stay inside these ranges and needn't reach their ends.
All inputs are finite; a program needn't handle non-finite values.
Results may differ from the reference program's by a relative error of at most 0.017.
The reference program's roundings to bfloat16 on the way count: a program that leaves them out, or rounds other values in their place, can miss the bound.
Values may be sent and summed in bfloat16 or wider, within the bound.
A program may use at most 128 MiB of HBM per device.

```python
import math
import jax
import jax.numpy as jnp
from jax import lax

C = 1536
HEADS = 8
KEY = 64
VAL = 192
CONV_DILATION = 64
SEQS = 2
LEN = 8192
N_TENSOR = 4


def draw_projection(key):
    sigma = C ** (-0.5)
    values = jnp.clip(jax.random.normal(key, (C, HEADS * KEY), jnp.float32), -4.0, 4.0) * sigma
    return values.astype(jnp.bfloat16)


def draw_query_weight(key, part):
    return draw_projection(jax.random.fold_in(key, 11))


def draw_key_weight(key, part):
    return draw_projection(jax.random.fold_in(key, 23))


def level_of(stream_key, extent, split, least, largest):
    loudness = 1.0
    for position, blocks in split:
        draws = jax.random.uniform(jax.random.fold_in(jax.random.fold_in(stream_key, 6), position), (blocks,), jnp.float32, least / len(split), largest / len(split))
        loudness = loudness * jnp.repeat(jnp.exp(draws), extent[position] // blocks).reshape((-1,) + (1,) * (len(extent) - 1 - position))
    return loudness


def scatter_about(key, dims, width, most, shards=(), dtype=jnp.bfloat16):
    entries = width * jax.random.normal(key, dims, jnp.float32)
    if shards:
        entries = entries * level_of(key, dims, shards, -0.22, 0.18)
    return jnp.clip(entries, -most, most).astype(dtype)


def setup_inputs(seed: int = 0) -> dict:
    seeds = jax.random.split(jax.random.key(seed), 8)
    return {
        "tokens_in": scatter_about(seeds[0], (SEQS, LEN, C), 1.0, 6.0, ((1, 64), (2, 4))),
        "query_weight": draw_query_weight(jax.random.fold_in(seeds[7], 71), 0),
        "key_weight": draw_key_weight(jax.random.fold_in(seeds[7], 71), 0),
        "value_weight": scatter_about(seeds[3], (C, HEADS * VAL), C ** -0.5, 0.15625, ((1, 4),)),
        "out_weight": scatter_about(seeds[4], (HEADS * VAL, C), (HEADS * VAL // 64) ** -0.5, 1.25, ((0, 4),)),
        "conv_weight": scatter_about(seeds[5], (3, C, C), (3 * C) ** -0.5, 0.09375, ((2, 4),)),
        "cotangent": scatter_about(seeds[6], (SEQS, LEN, C), 1.0, 6.0, ((1, 64), (2, 4))),
    }


eps_norm = 1e-05
root_half = 0.7071067811865476
inv_root_two_pi = 0.3989422804014327

def normalize(values):
    average = lax.optimization_barrier(jnp.mean(values, axis=-1, keepdims=True))
    centred = values - average
    inv_spread = lax.rsqrt(lax.optimization_barrier(jnp.mean(centred * centred, axis=-1, keepdims=True)) + eps_norm)
    return (centred * inv_spread, inv_spread)

def gelu_exact(values):
    return 0.5 * values * (1.0 + lax.erf(values * root_half))

def gelu_slope(values):
    return 0.5 * (1.0 + lax.erf(values * root_half)) + values * inv_root_two_pi * jnp.exp(-0.5 * values * values)

def reference(tokens_in, query_weight, key_weight, value_weight, out_weight, conv_weight, cotangent):
    seq_count, window_length, channel_width = tokens_in.shape
    row_indices = seq_count * window_length
    normed, _ = normalize(tokens_in.astype(jnp.float32))
    hidden = normed.astype(jnp.bfloat16).reshape(row_indices, channel_width)

    def project(weight, head_size):
        made = jnp.dot(hidden, weight, preferred_element_type=jnp.float32).astype(jnp.bfloat16)
        made = made.reshape(seq_count, window_length, HEADS, head_size).transpose(0, 2, 1, 3)
        return made.reshape(seq_count * HEADS, window_length, head_size)
    queries = project(query_weight, KEY)
    keys = project(key_weight, KEY)
    values_all = project(value_weight, VAL)
    block = math.gcd(window_length, 512)
    score_scale = KEY ** (-0.5)

    def one_head(operands):
        query_rows, key_rows, value_rows = operands

        def one_block(query_block):
            scores = jnp.dot(query_block, key_rows.T, preferred_element_type=jnp.float32) * score_scale
            top_score = lax.optimization_barrier(jnp.max(scores, axis=-1, keepdims=True))
            weights = jnp.exp(scores - top_score)
            totals = lax.optimization_barrier(jnp.sum(weights, axis=-1, keepdims=True))
            accum = jnp.dot(weights.astype(jnp.bfloat16), value_rows, preferred_element_type=jnp.float32)
            return (accum / totals).astype(jnp.bfloat16)
        return lax.map(one_block, query_rows.reshape(window_length // block, block, KEY)).reshape(window_length, VAL)
    attended = lax.map(one_head, (queries, keys, values_all))
    attended = attended.reshape(seq_count, HEADS, window_length, VAL).transpose(0, 2, 1, 3).reshape(row_indices, HEADS * VAL)
    mixed = jnp.dot(attended, out_weight, preferred_element_type=jnp.float32).reshape(seq_count, window_length, channel_width)
    block_in = (tokens_in.astype(jnp.float32) + mixed).astype(jnp.bfloat16)
    unit_normed, unit_inv = normalize(block_in.astype(jnp.float32))
    gelu_applied = gelu_exact(unit_normed).astype(jnp.bfloat16)
    units_padded = jnp.pad(gelu_applied, ((0, 0), (CONV_DILATION, CONV_DILATION), (0, 0)))
    kernel_offsets = [units_padded[:, kernel_offset * CONV_DILATION:kernel_offset * CONV_DILATION + window_length].reshape(row_indices, channel_width) for kernel_offset in range(3)]
    conv_out = jnp.zeros((row_indices, channel_width), jnp.float32)
    for kernel_offset in range(3):
        conv_out = conv_out + jnp.dot(kernel_offsets[kernel_offset], conv_weight[kernel_offset], preferred_element_type=jnp.float32)
    block_out = (block_in.astype(jnp.float32) + conv_out.reshape(seq_count, window_length, channel_width)).astype(jnp.bfloat16)
    grad_rows = cotangent.reshape(row_indices, channel_width)
    position_scale = (seq_count * window_length) ** (-0.5)
    kernel_terms = jnp.stack([jnp.dot(kernel_offsets[kernel_offset].T, grad_rows, preferred_element_type=jnp.float32) for kernel_offset in range(3)])
    conv_grad = (kernel_terms * position_scale).astype(jnp.bfloat16)
    gradient_padded = jnp.pad(cotangent, ((0, 0), (CONV_DILATION, CONV_DILATION), (0, 0)))
    kernel_tap_gradient = [gradient_padded[:, (2 - kernel_offset) * CONV_DILATION:(2 - kernel_offset) * CONV_DILATION + window_length].reshape(row_indices, channel_width) for kernel_offset in range(3)]
    group = channel_width // N_TENSOR
    unit_grad = jnp.zeros((row_indices, channel_width), jnp.float32)
    for part_index in range(N_TENSOR):
        first_col = part_index * group
        group_term = jnp.zeros((row_indices, channel_width), jnp.float32)
        for kernel_offset in range(3):
            group_term = group_term + jnp.dot(kernel_tap_gradient[kernel_offset][:, first_col:first_col + group], conv_weight[kernel_offset][:, first_col:first_col + group].T, preferred_element_type=jnp.float32)
        unit_grad = unit_grad + lax.optimization_barrier(group_term.astype(jnp.bfloat16)).astype(jnp.float32)
    unit_grad = unit_grad.reshape(seq_count, window_length, channel_width)
    slope_grad = unit_grad * gelu_slope(unit_normed)
    first_mean = lax.optimization_barrier(jnp.mean(slope_grad, axis=-1, keepdims=True))
    second_mean = lax.optimization_barrier(jnp.mean(slope_grad * unit_normed, axis=-1, keepdims=True))
    input_grad = (slope_grad - first_mean - unit_normed * second_mean) * unit_inv
    residual_grad = (cotangent.astype(jnp.float32) + input_grad).astype(jnp.bfloat16)
    return (block_out, conv_grad, residual_grad)
```

```python
import functools

import jax
import jax.numpy as jnp
from jax import lax
from jax.experimental import pallas as pl
from jax.experimental.pallas import tpu as pltpu
from jax.sharding import PartitionSpec as P

KEY = 64
VAL = 192
CONV_DILATION = 64
NT = 4
NX, NY, NZ, NC = 4, 4, 2, 2

eps_norm = 1e-05
root_half = 0.7071067811865476
inv_root_two_pi = 0.3989422804014327

MESH = pl.DeviceIdType.MESH
BF = jnp.bfloat16
F32 = jnp.float32
VMEM = pltpu.VMEM
VSPEC = pl.BlockSpec(memory_space=pltpu.VMEM)
VMEM_LIMIT = 60 * 1024 * 1024


def normalize(values):
    average = jnp.mean(values, axis=-1, keepdims=True)
    centred = values - average
    inv_spread = lax.rsqrt(jnp.mean(centred * centred, axis=-1, keepdims=True) + eps_norm)
    return (centred * inv_spread, inv_spread)


def gelu_exact(values):
    return 0.5 * values * (1.0 + lax.erf(values * root_half))


def gelu_slope(values):
    return 0.5 * (1.0 + lax.erf(values * root_half)) + values * inv_root_two_pi * jnp.exp(
        -0.5 * values * values
    )


def seq_pos():
    s = lax.axis_index("seq")
    core = lax.rem(s, 2)
    z = lax.rem(lax.div(s, 2), 2)
    y = lax.rem(lax.div(s, 4), 4)
    x = lax.div(s, 16)
    return x, y, z, core


def seq_dev(x, y, z, core):
    return ((x * NY + y) * NZ + z) * NC + core


def nxt(i, k):
    return lax.rem(i + k, 4)


class Sender:
    def __init__(self, send_sems, recv_sems):
        self.ss, self.rs, self.n, self.flying = send_sems, recv_sems, 0, []

    def make(self, src, dst, dev):
        i = self.n
        self.n += 1
        return pltpu.make_async_remote_copy(
            src_ref=src,
            dst_ref=dst,
            send_sem=self.ss.at[i],
            recv_sem=self.rs.at[i],
            device_id=dev,
            device_id_type=MESH,
        )

    def go(self, src, dst, dev):
        c = self.make(src, dst, dev)
        c.start()
        self.flying.append(c)
        return c

    def drain(self):
        for c in self.flying:
            c.wait_send()
        self.flying = []


def greet(devs):
    barrier = pltpu.get_barrier_semaphore()
    for d in devs:
        pl.semaphore_signal(barrier, inc=1, device_id=d, device_id_type=MESH)
    pl.semaphore_wait(barrier, len(devs))


class Gather4:
    def __init__(self, sender, view, me, plus, minus, on_block=None):
        self.s, self.view, self.me, self.plus, self.minus = sender, view, me, plus, minus

    def begin(self):
        s, v, me = self.s, self.view, self.me
        self.c0 = s.go(v(me, 0), v(me, 0), self.plus)
        self.c2 = s.go(v(me, 1), v(me, 1), self.minus)
        self.c1 = s.go(v(me, 1), v(me, 1), self.plus)
        self.c3 = s.go(v(me, 0), v(me, 0), self.minus)

    def relay(self):
        s, v, me = self.s, self.view, self.me
        self.c0.wait_recv()
        self.c4 = s.go(v(nxt(me, 3), 0), v(nxt(me, 3), 0), self.plus)
        self.c2.wait_recv()
        self.c5 = s.go(v(nxt(me, 1), 1), v(nxt(me, 1), 1), self.minus)

    def wait_near(self):
        self.c1.wait_recv()
        self.c3.wait_recv()

    def wait_far(self):
        self.c4.wait_recv()
        self.c5.wait_recv()


class Reduce4:
    def __init__(self, sender, x, rbuf, me, plus, minus):
        self.s, self.x, self.r, self.me, self.plus, self.minus = sender, x, rbuf, me, plus, minus

    def begin(self):
        s, x, r, me = self.s, self.x, self.r, self.me
        self.a0 = s.go(x(nxt(me, 2), 0), r(0, 0), self.plus)
        self.a1 = s.go(x(nxt(me, 2), 1), r(1, 1), self.minus)
        self.b0 = s.go(x(nxt(me, 1), 1), r(2, 1), self.plus)
        self.b1 = s.go(x(nxt(me, 3), 0), r(3, 0), self.minus)

    def combine(self):
        s, x, r, me = self.s, self.x, self.r, self.me
        self.a0.wait_recv()
        t0 = r(6, 0)
        t0[...] = (x(nxt(me, 1), 0)[...].astype(F32) + r(0, 0)[...].astype(F32)).astype(BF)
        self.c0 = s.go(t0, r(4, 0), self.plus)
        self.a1.wait_recv()
        t1 = r(7, 1)
        t1[...] = (x(nxt(me, 3), 1)[...].astype(F32) + r(1, 1)[...].astype(F32)).astype(BF)
        self.c1 = s.go(t1, r(5, 1), self.minus)

    def finish(self):
        x, r, me = self.x, self.r, self.me
        self.b0.wait_recv()
        self.b1.wait_recv()
        self.c0.wait_recv()
        h0 = x(me, 0)[...].astype(F32) + r(3, 0)[...].astype(F32) + r(4, 0)[...].astype(F32)
        self.c1.wait_recv()
        h1 = x(me, 1)[...].astype(F32) + r(2, 1)[...].astype(F32) + r(5, 1)[...].astype(F32)
        return h0, h1


def tensor_ring():
    t = lax.axis_index("tensor")
    return t, {"tensor": nxt(t, 1)}, {"tensor": nxt(t, 3)}


def params(cid):
    return pltpu.CompilerParams(
        collective_id=cid, has_side_effects=True, vmem_limit_bytes=VMEM_LIMIT
    )


def project_kernel(tok_ref, wq_ref, wk_ref, wv_ref, q_ref, kv_ref, full, ss, rs):
    t, plus, minus = tensor_ring()
    rows, width = tok_ref.shape
    half = rows // 2
    greet([plus, minus])

    def view(slot, h):
        return full.at[slot, pl.ds(h * half, half)]

    full[t] = tok_ref[...]
    s = Sender(ss, rs)
    g = Gather4(s, view, t, plus, minus)
    g.begin()
    g.relay()
    g.wait_near()
    g.wait_far()
    values = jnp.concatenate([full[i] for i in range(NT)], axis=1).astype(F32)
    hidden = normalize(values)[0].astype(BF)
    q_ref[...] = jnp.dot(hidden, wq_ref[...], preferred_element_type=F32).astype(BF)
    keys = q_ref.shape[1]
    kv_ref[:, :keys] = jnp.dot(hidden, wk_ref[...], preferred_element_type=F32).astype(BF)
    kv_ref[:, keys:] = jnp.dot(hidden, wv_ref[...], preferred_element_type=F32).astype(BF)
    s.drain()


def project(tokens, wq, wk, wv):
    rows, width = tokens.shape
    return pl.pallas_call(
        project_kernel,
        name="project",
        out_shape=(
            jax.ShapeDtypeStruct((rows, wq.shape[1]), BF),
            jax.ShapeDtypeStruct((rows, wk.shape[1] + wv.shape[1]), BF),
        ),
        in_specs=[VSPEC] * 4,
        out_specs=(VSPEC, VSPEC),
        scratch_shapes=[
            VMEM((NT, rows, width), BF),
            pltpu.SemaphoreType.DMA((6,)),
            pltpu.SemaphoreType.DMA((6,)),
        ],
        compiler_params=params(1),
    )(tokens, wq, wk, wv)


def attention_kernel(q_ref, kv_ref, out_ref, qbuf, kvbuf, obuf, orecv, lbuf, lrecv, ss, rs):
    x, y, z, core = seq_pos()
    count = q_ref.shape[1]
    partner = {"seq": seq_dev(x, y, z, 1 - core)}
    zpeer = {"seq": seq_dev(x, y, 1 - z, core)}
    xs = [{"seq": seq_dev(nxt(x, k), y, z, core)} for k in (1, 2, 3)]
    ys = [{"seq": seq_dev(x, nxt(y, k), z, core)} for k in (1, 2, 3)]
    greet([partner, zpeer] + xs + ys)
    s = Sender(ss, rs)
    half = count // 2
    axes = ((x, xs, y, ys), (y, ys, x, xs))
    state = []
    for i, (a, a_dev, b, b_dev) in enumerate(axes):
        kvbuf[i, a, z, core] = kv_ref[i]
        qbuf[i, b] = q_ref[i]

    for i, (a, a_dev, b, b_dev) in enumerate(axes):
        own = kvbuf.at[i, a, z, core]
        cz = s.go(own, own, zpeer)

        def kview(slot, h, i=i, zz=z):
            return kvbuf.at[i, slot, zz, core, pl.ds(h * half, half)]

        def oview(slot, h, i=i, zz=1 - z):
            return kvbuf.at[i, slot, zz, core, pl.ds(h * half, half)]

        def qview(slot, h, i=i):
            return qbuf.at[i, slot, pl.ds(h * half, half)]

        gk = Gather4(s, kview, a, a_dev[0], a_dev[2])
        go = Gather4(s, oview, a, a_dev[0], a_dev[2])
        gq = Gather4(s, qview, b, b_dev[0], b_dev[2])
        gq.begin()
        gk.begin()
        fw = [s.go(own, own, partner)]
        state.append((cz, gk, go, gq, fw))
    for i, (a, a_dev, b, b_dev) in enumerate(axes):
        cz, gk, go, gq, fw = state[i]
        cz.wait_recv()
        go.begin()
        mine = kvbuf.at[i, a, 1 - z, core]
        fw.append(s.go(mine, mine, partner))
        gq.relay()
        gk.relay()
    for i, (a, a_dev, b, b_dev) in enumerate(axes):
        cz, gk, go, gq, fw = state[i]
        gk.wait_near()
        for k in (1, 3):
            ref = kvbuf.at[i, nxt(a, k), z, core]
            fw.append(s.go(ref, ref, partner))
        go.relay()
        gk.wait_far()
        ref = kvbuf.at[i, nxt(a, 2), z, core]
        fw.append(s.go(ref, ref, partner))
    for i, (a, a_dev, b, b_dev) in enumerate(axes):
        cz, gk, go, gq, fw = state[i]
        go.wait_near()
        for k in (1, 3):
            ref = kvbuf.at[i, nxt(a, k), 1 - z, core]
            fw.append(s.go(ref, ref, partner))
        go.wait_far()
        ref = kvbuf.at[i, nxt(a, 2), 1 - z, core]
        fw.append(s.go(ref, ref, partner))
        gq.wait_near()
        gq.wait_far()
    lane = lax.broadcasted_iota(jnp.int32, (count, 128), 1)
    scale = KEY ** (-0.5)
    keys = NX * NZ * NC * count
    sent = []
    for i, (a, a_dev, b, b_dev) in enumerate(axes):
        for f in state[i][4]:
            f.wait_recv()

        @pl.loop(0, 4)
        def _(r, i=i):
            q = qbuf[i, r]
            k = kvbuf[i, :, :, :, :, 0:128].reshape(keys, 128)
            parts = []
            stats = jnp.zeros((count, 128), F32)
            for h in range(2):
                qh = jnp.where((lane < KEY) if h == 0 else (lane >= KEY), q, jnp.zeros_like(q))
                sc = (
                    lax.dot_general(
                        qh, k, (((1,), (1,)), ((), ())), preferred_element_type=F32
                    )
                    * scale
                )
                top = jnp.max(sc, axis=-1, keepdims=True)
                w = jnp.exp(sc - top)
                total = jnp.sum(w, axis=-1, keepdims=True)
                v = kvbuf[i, :, :, :, :, 128 + 128 * h : 384 + 128 * h].reshape(keys, 256)
                acc = jnp.dot(w.astype(BF), v, preferred_element_type=F32) / total
                parts.append(acc)
                stats = jnp.where(lane == h, top + jnp.log(total), stats)
            obuf[i, r, :, 0:128] = parts[0][:, :128].astype(BF)
            obuf[i, r, :, 128:256] = jnp.where(
                lane < 64, parts[0][:, 128:], parts[1][:, :128]
            ).astype(BF)
            obuf[i, r, :, 256:384] = parts[1][:, 128:].astype(BF)
            lbuf[i, r] = stats.T[0:8]

        for k in (2, 1, 3):
            dev = b_dev[k - 1]
            sent.append(s.go(obuf.at[i, nxt(b, k)], orecv.at[i, b], dev))
            sent.append(s.go(lbuf.at[i, nxt(b, k)], lrecv.at[i, b], dev))
        orecv[i, b] = obuf[i, b]
        lrecv[i, b] = lbuf[i, b]
    for c in sent:
        c.wait_recv()
    for i in range(2):
        logs = []
        for r in range(4):
            wide = jnp.concatenate([lrecv[i, r], jnp.zeros((120, 128), F32)], axis=0).T
            logs.append([wide[:, h : h + 1] for h in range(2)])
        wts = []
        for h in range(2):
            top = logs[0][h]
            for r in range(1, 4):
                top = jnp.maximum(top, logs[r][h])
            e = [jnp.exp(logs[r][h] - top) for r in range(4)]
            total = e[0] + e[1] + e[2] + e[3]
            wts.append([er / total for er in e])
        for g in range(3):
            acc = jnp.zeros((count, 128), F32)
            for r in range(4):
                if g == 0:
                    w = wts[0][r]
                elif g == 2:
                    w = wts[1][r]
                else:
                    w = jnp.where(lane < 64, wts[0][r], wts[1][r])
                acc = acc + orecv[i, r, :, 128 * g : 128 * g + 128].astype(F32) * w
            out_ref[i, :, 128 * g : 128 * g + 128] = acc.astype(BF)
    s.drain()


def attention(q, kv):
    seqs, count, keys = q.shape
    vals = kv.shape[2] - keys
    n = 2 * (1 + 6 * 3 + 8 + 6)
    return pl.pallas_call(
        attention_kernel,
        name="attention",
        out_shape=jax.ShapeDtypeStruct((seqs, count, vals), BF),
        in_specs=[VSPEC] * 2,
        out_specs=VSPEC,
        scratch_shapes=[
            VMEM((seqs, 4, count, keys), BF),
            VMEM((seqs, 4, NZ, NC, count, keys + vals), BF),
            VMEM((seqs, 4, count, vals), BF),
            VMEM((seqs, 4, count, vals), BF),
            VMEM((seqs, 4, 8, count), F32),
            VMEM((seqs, 4, 8, count), F32),
            pltpu.SemaphoreType.DMA((n,)),
            pltpu.SemaphoreType.DMA((n,)),
        ],
        compiler_params=params(2),
    )(q, kv)


def tensor_sum_kernel(terms_ref, *refs, has_base):
    if has_base:
        base_ref, out_ref, rbuf, ss, rs = refs
    else:
        out_ref, rbuf, ss, rs = refs
    t, plus, minus = tensor_ring()
    rows = terms_ref.shape[1]
    half = rows // 2
    greet([plus, minus])
    s = Sender(ss, rs)

    def x(p, h):
        return terms_ref.at[p, pl.ds(h * half, half)]

    red = Reduce4(s, x, lambda i, h: rbuf.at[i], t, plus, minus)
    red.begin()
    red.combine()
    parts = red.finish()
    for h in range(2):
        part = parts[h]
        if has_base:
            part = part + base_ref[h * half : (h + 1) * half].astype(F32)
        out_ref[t, pl.ds(h * half, half)] = part.astype(BF)
    g = Gather4(s, lambda p, h: out_ref.at[p, pl.ds(h * half, half)], t, plus, minus)
    g.begin()
    g.relay()
    g.wait_near()
    g.wait_far()
    s.drain()


def tensor_sum(terms, base, cid):
    _, rows, width = terms.shape
    args = (terms,) if base is None else (terms, base)
    return pl.pallas_call(
        functools.partial(tensor_sum_kernel, has_base=base is not None),
        name="tensor_sum_%d" % cid,
        out_shape=jax.ShapeDtypeStruct(terms.shape, BF),
        in_specs=[VSPEC] * len(args),
        out_specs=VSPEC,
        scratch_shapes=[
            VMEM((8, rows // 2, width), BF),
            pltpu.SemaphoreType.DMA((12,)),
            pltpu.SemaphoreType.DMA((12,)),
        ],
        compiler_params=params(cid),
    )(*args)


def conv_grad_kernel(
    units_ref, cot_ref, out_ref, send, recv, sums, r1, mid, r2, fin, zrecv, ss, rs
):
    x, y, z, core = seq_pos()
    width = units_ref.shape[1]
    total = 3 * width
    mine = total // 2
    tile = 256
    tiles = mine // tile
    per_tap = width // tile

    def pick(u, v):
        return jnp.where(core == 0, u, v)

    a, b = pick(x, y), pick(y, x)

    def along_a(k):
        return {"seq": pick(seq_dev(nxt(x, k), y, z, core), seq_dev(x, nxt(y, k), z, core))}

    def along_b(k):
        return {"seq": pick(seq_dev(x, nxt(y, k), z, core), seq_dev(nxt(x, k), y, z, core))}

    partner = {"seq": seq_dev(x, y, z, 1 - core)}
    zpeer = {"seq": seq_dev(x, y, 1 - z, core)}
    ap, am, bp, bm = along_a(1), along_a(3), along_b(1), along_b(3)
    greet([partner, zpeer, ap, am, bp, bm])

    def product(g):
        tap = lax.div(g, per_tap)
        col = pl.multiple_of(lax.rem(g, per_tap) * tile, tile)
        return lax.dot_general(
            units_ref[:, pl.ds(col, tile)],
            cot_ref[tap],
            (((0,), (0,)), ((), ())),
            preferred_element_type=F32,
        )

    def exchange(i):
        return pltpu.make_async_remote_copy(
            src_ref=send.at[i],
            dst_ref=recv.at[i],
            send_sem=ss.at[i],
            recv_sem=rs.at[i],
            device_id=partner,
            device_id_type=MESH,
        )

    @pl.loop(0, tiles)
    def _(i):
        send[i] = product((1 - core) * tiles + i).astype(BF)
        exchange(i).start()

    @pl.loop(0, tiles)
    def _(i):
        own = product(core * tiles + i)
        exchange(i).wait_recv()
        row = pl.multiple_of(i * tile, tile)
        sums[pl.ds(row, tile)] = (own + recv[i].astype(F32)).astype(BF)

    s = Sender(ss, rs)
    s.n = tiles
    big = mine // 4
    small = big // 4
    bh = (0, big // 2)
    bn = (big // 2, big // 2)
    cut = (small // 2 + 15) // 16 * 16
    sh = (0, cut)
    sn = (cut, small - cut)

    def m16(v):
        return pl.multiple_of(v, 16)

    first = Reduce4(
        s,
        lambda p, h: sums.at[pl.ds(m16(p * big + bh[h]), bn[h])],
        lambda i, h: r1.at[i],
        a,
        ap,
        am,
    )
    first.begin()
    first.combine()
    h0, h1 = first.finish()
    mid[0 : big // 2] = h0.astype(BF)
    mid[big // 2 : big] = h1.astype(BF)
    second = Reduce4(
        s,
        lambda p, h: mid.at[pl.ds(m16(p * small + sh[h]), sn[h])],
        lambda i, h: r2.at[i, pl.ds(0, sn[h])],
        b,
        bp,
        bm,
    )
    second.begin()
    second.combine()
    h0, h1 = second.finish()
    fin[0:cut] = h0.astype(BF)
    fin[cut:small] = h1.astype(BF)
    cz = s.go(fin, zrecv, zpeer)
    cz.wait_recv()
    at = core * mine + a * big + b * small
    out_ref[pl.ds(m16(at), small)] = (fin[...].astype(F32) + zrecv[...].astype(F32)).astype(BF)
    g2 = Gather4(
        s,
        lambda p, h: out_ref.at[pl.ds(m16(core * mine + a * big + p * small + sh[h]), sn[h])],
        b,
        bp,
        bm,
    )
    g2.begin()
    g2.relay()
    g2.wait_near()
    g2.wait_far()

    def block(p):
        return out_ref.at[pl.ds(m16(core * mine + p * big), big)]

    g1 = Gather4(
        s,
        lambda p, h: out_ref.at[pl.ds(m16(core * mine + p * big + bh[h]), bn[h])],
        a,
        ap,
        am,
    )
    g1.begin()
    fw = [s.go(block(a), block(a), partner)]
    g1.relay()
    g1.wait_near()
    for k in (1, 3):
        fw.append(s.go(block(nxt(a, k)), block(nxt(a, k)), partner))
    g1.wait_far()
    fw.append(s.go(block(nxt(a, 2)), block(nxt(a, 2)), partner))
    for f in fw:
        f.wait_recv()
    s.drain()

    @pl.loop(0, tiles)
    def _(i):
        exchange(i).wait_send()


def conv_grad_sum(units, cots):
    rows, width = units.shape
    local = cots.shape[2]
    mine = 3 * width // 2
    big, small = mine // 4, mine // 16
    cut = (small // 2 + 15) // 16 * 16
    n = mine // 256 + 6 * 4 + 1 + 4
    return pl.pallas_call(
        conv_grad_kernel,
        name="conv_grad",
        out_shape=jax.ShapeDtypeStruct((3 * width, local), BF),
        in_specs=[VSPEC] * 2,
        out_specs=VSPEC,
        scratch_shapes=[
            VMEM((mine // 256, 256, local), BF),
            VMEM((mine // 256, 256, local), BF),
            VMEM((mine, local), BF),
            VMEM((8, big // 2, local), BF),
            VMEM((big, local), BF),
            VMEM((8, cut, local), BF),
            VMEM((small, local), BF),
            VMEM((small, local), BF),
            pltpu.SemaphoreType.DMA((n,)),
            pltpu.SemaphoreType.DMA((n,)),
        ],
        compiler_params=params(5),
    )(units, cots)


def from_neighbours(head, tail, axis):
    count = lax.axis_size(axis)
    ends = count - 1
    before = lax.ppermute(tail, axis, [(i, i + 1) for i in range(ends)])
    after = lax.ppermute(head, axis, [(i + 1, i) for i in range(ends)])
    return before, after


def body(tokens_in, query_weight, key_weight, value_weight, out_weight, conv_weight, cotangent):
    seqs, count, local = tokens_in.shape
    width = local * NT
    rows = seqs * count
    edge = CONV_DILATION
    q, kv = project(tokens_in.reshape(rows, local), query_weight, key_weight, value_weight)
    attended = attention(q.reshape(seqs, count, -1), kv.reshape(seqs, count, -1))

    before, after = from_neighbours(cotangent[:, :edge], cotangent[:, count - edge :], "seq")
    cot_ext = jnp.concatenate([before, cotangent, after], axis=1)
    cots = jnp.stack(
        [
            cot_ext[:, (2 - j) * edge : (2 - j) * edge + count].reshape(rows, local)
            for j in range(3)
        ]
    )
    unit_terms = jnp.einsum("jrk,jck->rc", cots, conv_weight, preferred_element_type=F32)
    unit_terms = unit_terms.astype(BF).reshape(rows, NT, local).transpose(1, 0, 2)
    unit_grad = tensor_sum(unit_terms, None, 3)

    mixed = jnp.dot(attended.reshape(rows, local), out_weight, preferred_element_type=F32)
    mixed = mixed.astype(BF).reshape(rows, NT, local).transpose(1, 0, 2)
    block_full = tensor_sum(mixed, tokens_in.reshape(rows, local), 4)
    t = lax.axis_index("tensor")
    block_in = lax.dynamic_index_in_dim(block_full, t, 0, keepdims=False)
    block_full = block_full.transpose(1, 0, 2).reshape(rows, width)
    unit_normed, unit_inv = normalize(block_full.astype(F32))
    units = gelu_exact(unit_normed).astype(BF)

    conv_grad = conv_grad_sum(units, cots)
    conv_grad = (conv_grad.astype(F32) * ((rows * lax.axis_size("seq")) ** (-0.5))).astype(BF)
    conv_grad = conv_grad.reshape(3, width, local)

    taps = [
        jnp.dot(units, conv_weight[j], preferred_element_type=F32).reshape(seqs, count, local)
        for j in range(3)
    ]
    before, after = from_neighbours(taps[2][:, :edge], taps[0][:, count - edge :], "seq")
    from_left = jnp.concatenate([before, taps[0][:, : count - edge]], axis=1)
    from_right = jnp.concatenate([taps[2][:, edge:], after], axis=1)
    conv_out = from_left + taps[1] + from_right
    block_out = (block_in.reshape(seqs, count, local).astype(F32) + conv_out).astype(BF)

    unit_grad = unit_grad.transpose(1, 0, 2).reshape(rows, width).astype(F32)
    slope_grad = unit_grad * gelu_slope(unit_normed)
    first_mean = jnp.sum(slope_grad, axis=-1, keepdims=True) / width
    second_mean = jnp.sum(slope_grad * unit_normed, axis=-1, keepdims=True) / width
    full_grad = (slope_grad - first_mean - unit_normed * second_mean) * unit_inv
    input_grad = lax.dynamic_slice_in_dim(full_grad, t * local, local, 1)
    residual_grad = (cotangent.astype(F32) + input_grad.reshape(seqs, count, local)).astype(BF)
    return (block_out, conv_grad, residual_grad)


def solution(mesh):
    placed = (
        P(None, "seq", "tensor"),
        P(None, "tensor"),
        P(None, "tensor"),
        P(None, "tensor"),
        P("tensor", None),
        P(None, None, "tensor"),
        P(None, "seq", "tensor"),
    )
    return jax.shard_map(
        body,
        mesh=mesh,
        in_specs=placed,
        out_specs=(P(None, "seq", "tensor"), P(None, None, "tensor"), P(None, "seq", "tensor")),
        check_vma=False,
    )
```

```python
import functools

import jax
import jax.numpy as jnp
from jax import lax
from jax.experimental import pallas as pl
from jax.experimental.pallas import tpu as pltpu
from jax.sharding import PartitionSpec as P

KEY = 64
VAL = 192
CONV_DILATION = 64
NT = 4
NX, NY, NZ, NC = 4, 4, 2, 2

eps_norm = 1e-05
root_half = 0.7071067811865476
inv_root_two_pi = 0.3989422804014327

MESH = pl.DeviceIdType.MESH
BF = jnp.bfloat16
F32 = jnp.float32
VMEM = pltpu.VMEM
VSPEC = pl.BlockSpec(memory_space=pltpu.VMEM)
HSPEC = pl.BlockSpec(memory_space=pltpu.HBM)


def normalize(values):
    average = jnp.mean(values, axis=-1, keepdims=True)
    centred = values - average
    inv_spread = lax.rsqrt(jnp.mean(centred * centred, axis=-1, keepdims=True) + eps_norm)
    return (centred * inv_spread, inv_spread)


def gelu_exact(values):
    return 0.5 * values * (1.0 + lax.erf(values * root_half))


def gelu_slope(values):
    return 0.5 * (1.0 + lax.erf(values * root_half)) + values * inv_root_two_pi * jnp.exp(
        -0.5 * values * values
    )


def seq_pos():
    s = lax.axis_index("seq")
    core = lax.rem(s, 2)
    z = lax.rem(lax.div(s, 2), 2)
    y = lax.rem(lax.div(s, 4), 4)
    x = lax.div(s, 16)
    return x, y, z, core


def seq_dev(x, y, z, core):
    return ((x * NY + y) * NZ + z) * NC + core


def nxt(i, k):
    return lax.rem(i + k, 4)


class Sender:
    def __init__(self, send_sems, recv_sems):
        self.ss, self.rs, self.n, self.flying = send_sems, recv_sems, 0, []

    def make(self, src, dst, dev):
        i = self.n
        self.n += 1
        return pltpu.make_async_remote_copy(
            src_ref=src,
            dst_ref=dst,
            send_sem=self.ss.at[i],
            recv_sem=self.rs.at[i],
            device_id=dev,
            device_id_type=MESH,
        )

    def go(self, src, dst, dev):
        c = self.make(src, dst, dev)
        c.start()
        self.flying.append(c)
        return c

    def drain(self):
        for c in self.flying:
            c.wait_send()
        self.flying = []


def greet(devs):
    barrier = pltpu.get_barrier_semaphore()
    for d in devs:
        pl.semaphore_signal(barrier, inc=1, device_id=d, device_id_type=MESH)
    pl.semaphore_wait(barrier, len(devs))


class Gather4:
    def __init__(self, sender, view, me, plus, minus, on_block=None):
        self.s, self.view, self.me, self.plus, self.minus = sender, view, me, plus, minus

    def begin(self):
        s, v, me = self.s, self.view, self.me
        self.c0 = s.go(v(me, 0), v(me, 0), self.plus)
        self.c2 = s.go(v(me, 1), v(me, 1), self.minus)
        self.c1 = s.go(v(me, 1), v(me, 1), self.plus)
        self.c3 = s.go(v(me, 0), v(me, 0), self.minus)

    def relay(self):
        s, v, me = self.s, self.view, self.me
        self.c0.wait_recv()
        self.c4 = s.go(v(nxt(me, 3), 0), v(nxt(me, 3), 0), self.plus)
        self.c2.wait_recv()
        self.c5 = s.go(v(nxt(me, 1), 1), v(nxt(me, 1), 1), self.minus)

    def wait_near(self):
        self.c1.wait_recv()
        self.c3.wait_recv()

    def wait_far(self):
        self.c4.wait_recv()
        self.c5.wait_recv()


class Reduce4:
    def __init__(self, sender, x, rbuf, me, plus, minus):
        self.s, self.x, self.r, self.me, self.plus, self.minus = sender, x, rbuf, me, plus, minus

    def begin(self):
        s, x, r, me = self.s, self.x, self.r, self.me
        self.a0 = s.go(x(nxt(me, 2), 0), r(0, 0), self.plus)
        self.a1 = s.go(x(nxt(me, 2), 1), r(1, 1), self.minus)
        self.b0 = s.go(x(nxt(me, 1), 1), r(2, 1), self.plus)
        self.b1 = s.go(x(nxt(me, 3), 0), r(3, 0), self.minus)

    def combine(self):
        s, x, r, me = self.s, self.x, self.r, self.me
        self.a0.wait_recv()
        t0 = r(6, 0)
        t0[...] = (x(nxt(me, 1), 0)[...].astype(F32) + r(0, 0)[...].astype(F32)).astype(BF)
        self.c0 = s.go(t0, r(4, 0), self.plus)
        self.a1.wait_recv()
        t1 = r(7, 1)
        t1[...] = (x(nxt(me, 3), 1)[...].astype(F32) + r(1, 1)[...].astype(F32)).astype(BF)
        self.c1 = s.go(t1, r(5, 1), self.minus)

    def finish(self):
        x, r, me = self.x, self.r, self.me
        self.b0.wait_recv()
        self.b1.wait_recv()
        self.c0.wait_recv()
        h0 = x(me, 0)[...].astype(F32) + r(3, 0)[...].astype(F32) + r(4, 0)[...].astype(F32)
        self.c1.wait_recv()
        h1 = x(me, 1)[...].astype(F32) + r(2, 1)[...].astype(F32) + r(5, 1)[...].astype(F32)
        return h0, h1


def tensor_ring():
    t = lax.axis_index("tensor")
    return t, {"tensor": nxt(t, 1)}, {"tensor": nxt(t, 3)}


def params(cid, mib):
    return pltpu.CompilerParams(
        collective_id=cid, has_side_effects=True, vmem_limit_bytes=mib * 1024 * 1024
    )


def seq_next(k):
    return {"seq": lax.rem(lax.axis_index("seq") + k, NX * NY * NZ * NC)}


def seq_prev():
    return seq_next(NX * NY * NZ * NC - 1)


def fetch(sem, i, src, dst):
    c = pltpu.make_async_copy(src, dst, sem.at[i])
    c.start()
    return c


def project_kernel(
    tok_ref, cot_ref, wq_hbm, wk_hbm, wv_hbm, cw_hbm,
    q_ref, kv_ref, cotx, terms_ref,
    full, wq, wk, wv, cw, cots, ss, rs, ls,
):
    t, plus, minus = tensor_ring()
    rows, width = tok_ref.shape
    half = rows // 2
    edge = CONV_DILATION
    count = cot_ref.shape[1]
    me = lax.axis_index("seq")
    last = NX * NY * NZ * NC - 1
    ccw = fetch(ls, 0, cw_hbm, cw)
    cw3 = [fetch(ls, 1, wq_hbm, wq), fetch(ls, 2, wk_hbm, wk), fetch(ls, 3, wv_hbm, wv)]
    full[t] = tok_ref[...]
    cotx[:, edge : edge + count] = cot_ref[...]
    greet([plus, minus, seq_next(1), seq_prev()])

    def view(slot, h):
        return full.at[slot, pl.ds(h * half, half)]

    s = Sender(ss, rs)
    g = Gather4(s, view, t, plus, minus)
    g.begin()
    up = s.go(cot_ref.at[:, count - edge : count], cotx.at[:, 0:edge], seq_next(1))
    down = s.go(cot_ref.at[:, 0:edge], cotx.at[:, edge + count : 2 * edge + count], seq_prev())
    up.wait_recv()
    down.wait_recv()

    @pl.when(me == 0)
    def _():
        cotx[:, 0:edge] = jnp.zeros((2, edge, width), BF)

    @pl.when(me == last)
    def _():
        cotx[:, edge + count : 2 * edge + count] = jnp.zeros((2, edge, width), BF)

    for j in range(3):
        cots[j] = cotx[:, (2 - j) * edge : (2 - j) * edge + count].reshape(rows, width)
    ccw.wait()

    def term(p):
        acc = jnp.zeros((rows, width), F32)
        for j in range(3):
            acc = acc + lax.dot_general(
                cots[j],
                cw[j, p * width : (p + 1) * width],
                (((1,), (1,)), ((), ())),
                preferred_element_type=F32,
            )
        terms_ref[p] = acc.astype(BF)

    term(0)
    g.relay()
    for p in range(1, NT):
        term(p)
    for c in cw3:
        c.wait()
    g.wait_near()
    g.wait_far()
    for h in range(2):
        at = slice(h * half, (h + 1) * half)
        values = jnp.concatenate([full[i, at] for i in range(NT)], axis=1).astype(F32)
        hidden = normalize(values)[0].astype(BF)
        q_ref[h] = jnp.dot(hidden, wq[...], preferred_element_type=F32).astype(BF)
        keys = q_ref.shape[2]
        kv_ref[h, :, :keys] = jnp.dot(hidden, wk[...], preferred_element_type=F32).astype(BF)
        kv_ref[h, :, keys:] = jnp.dot(hidden, wv[...], preferred_element_type=F32).astype(BF)
    s.drain()


def project(tokens, cot, wq, wk, wv, cw):
    rows, width = tokens.shape
    seqs, count, _ = cot.shape
    return pl.pallas_call(
        project_kernel,
        name="project",
        out_shape=(
            jax.ShapeDtypeStruct((seqs, count, wq.shape[1]), BF),
            jax.ShapeDtypeStruct((seqs, count, wk.shape[1] + wv.shape[1]), BF),
            jax.ShapeDtypeStruct((seqs, count + 2 * CONV_DILATION, width), BF),
            jax.ShapeDtypeStruct((NT, rows, width), BF),
        ),
        in_specs=[VSPEC] * 2 + [HSPEC] * 4,
        out_specs=(VSPEC,) * 4,
        scratch_shapes=[
            VMEM((NT, rows, width), BF),
            VMEM(wq.shape, BF),
            VMEM(wk.shape, BF),
            VMEM(wv.shape, BF),
            VMEM(cw.shape, BF),
            VMEM((3, rows, width), BF),
            pltpu.SemaphoreType.DMA((8,)),
            pltpu.SemaphoreType.DMA((8,)),
            pltpu.SemaphoreType.DMA((4,)),
        ],
        compiler_params=params(1, 32),
    )(tokens, cot, wq, wk, wv, cw)


def attention_kernel(
    q_ref, kv_ref, terms_ref, out_ref, ug_ref, rbuf, qbuf, kvbuf, obuf, orecv, lbuf, lrecv, ss, rs
):
    x, y, z, core = seq_pos()
    t, plus, minus = tensor_ring()
    count = q_ref.shape[1]
    partner = {"seq": seq_dev(x, y, z, 1 - core)}
    zpeer = {"seq": seq_dev(x, y, 1 - z, core)}
    xs = [{"seq": seq_dev(nxt(x, k), y, z, core)} for k in (1, 2, 3)]
    ys = [{"seq": seq_dev(x, nxt(y, k), z, core)} for k in (1, 2, 3)]
    greet([partner, zpeer, plus, minus] + xs + ys)
    s = Sender(ss, rs)
    half = count // 2
    axes = ((x, xs, y, ys), (y, ys, x, xs))
    state = []
    for i, (a, a_dev, b, b_dev) in enumerate(axes):
        kvbuf[i, a, z, core] = kv_ref[i]
        qbuf[i, b] = q_ref[i]

    for i, (a, a_dev, b, b_dev) in enumerate(axes):
        own = kvbuf.at[i, a, z, core]
        cz = s.go(own, own, zpeer)

        def kview(slot, h, i=i, zz=z):
            return kvbuf.at[i, slot, zz, core, pl.ds(h * half, half)]

        def oview(slot, h, i=i, zz=1 - z):
            return kvbuf.at[i, slot, zz, core, pl.ds(h * half, half)]

        def qview(slot, h, i=i):
            return qbuf.at[i, slot, pl.ds(h * half, half)]

        gk = Gather4(s, kview, a, a_dev[0], a_dev[2])
        go = Gather4(s, oview, a, a_dev[0], a_dev[2])
        gq = Gather4(s, qview, b, b_dev[0], b_dev[2])
        gq.begin()
        gk.begin()
        fw = [s.go(own, own, partner)]
        state.append((cz, gk, go, gq, fw))

    def term(p, h):
        return terms_ref.at[p, pl.ds(h * count, count)]

    red = Reduce4(s, term, lambda i, h: rbuf.at[i], t, plus, minus)
    red.begin()
    for i, (a, a_dev, b, b_dev) in enumerate(axes):
        cz, gk, go, gq, fw = state[i]
        cz.wait_recv()
        go.begin()
        mine = kvbuf.at[i, a, 1 - z, core]
        fw.append(s.go(mine, mine, partner))
        gq.relay()
        gk.relay()
    for i, (a, a_dev, b, b_dev) in enumerate(axes):
        cz, gk, go, gq, fw = state[i]
        gk.wait_near()
        for k in (1, 3):
            ref = kvbuf.at[i, nxt(a, k), z, core]
            fw.append(s.go(ref, ref, partner))
        go.relay()
        gk.wait_far()
        ref = kvbuf.at[i, nxt(a, 2), z, core]
        fw.append(s.go(ref, ref, partner))
    for i, (a, a_dev, b, b_dev) in enumerate(axes):
        cz, gk, go, gq, fw = state[i]
        go.wait_near()
        for k in (1, 3):
            ref = kvbuf.at[i, nxt(a, k), 1 - z, core]
            fw.append(s.go(ref, ref, partner))
        go.wait_far()
        ref = kvbuf.at[i, nxt(a, 2), 1 - z, core]
        fw.append(s.go(ref, ref, partner))
        gq.wait_near()
        gq.wait_far()
    red.combine()
    lane = lax.broadcasted_iota(jnp.int32, (count, 128), 1)
    scale = KEY ** (-0.5)
    keys = NX * NZ * NC * count
    sent = []
    for i, (a, a_dev, b, b_dev) in enumerate(axes):
        for f in state[i][4]:
            f.wait_recv()

        @pl.loop(0, 4)
        def _(r, i=i):
            q = qbuf[i, r]
            k = kvbuf[i, :, :, :, :, 0:128].reshape(keys, 128)
            parts = []
            stats = jnp.zeros((count, 128), F32)
            for h in range(2):
                qh = jnp.where((lane < KEY) if h == 0 else (lane >= KEY), q, jnp.zeros_like(q))
                sc = (
                    lax.dot_general(
                        qh, k, (((1,), (1,)), ((), ())), preferred_element_type=F32
                    )
                    * scale
                )
                top = jnp.max(sc, axis=-1, keepdims=True)
                w = jnp.exp(sc - top)
                total = jnp.sum(w, axis=-1, keepdims=True)
                v = kvbuf[i, :, :, :, :, 128 + 128 * h : 384 + 128 * h].reshape(keys, 256)
                acc = jnp.dot(w.astype(BF), v, preferred_element_type=F32) / total
                parts.append(acc)
                stats = jnp.where(lane == h, top + jnp.log(total), stats)
            obuf[i, r, :, 0:128] = parts[0][:, :128].astype(BF)
            obuf[i, r, :, 128:256] = jnp.where(
                lane < 64, parts[0][:, 128:], parts[1][:, :128]
            ).astype(BF)
            obuf[i, r, :, 256:384] = parts[1][:, 128:].astype(BF)
            lbuf[i, r] = stats.T[0:8]

        for k in (2, 1, 3):
            dev = b_dev[k - 1]
            sent.append(s.go(obuf.at[i, nxt(b, k)], orecv.at[i, b], dev))
            sent.append(s.go(lbuf.at[i, nxt(b, k)], lrecv.at[i, b], dev))
        orecv[i, b] = obuf[i, b]
        lrecv[i, b] = lbuf[i, b]
    parts = red.finish()
    for h in range(2):
        ug_ref[h * count : (h + 1) * count] = parts[h]
    for c in sent:
        c.wait_recv()
    for i in range(2):
        logs = []
        for r in range(4):
            wide = jnp.concatenate([lrecv[i, r], jnp.zeros((120, 128), F32)], axis=0).T
            logs.append([wide[:, h : h + 1] for h in range(2)])
        wts = []
        for h in range(2):
            top = logs[0][h]
            for r in range(1, 4):
                top = jnp.maximum(top, logs[r][h])
            e = [jnp.exp(logs[r][h] - top) for r in range(4)]
            total = e[0] + e[1] + e[2] + e[3]
            wts.append([er / total for er in e])
        for g in range(3):
            acc = jnp.zeros((count, 128), F32)
            for r in range(4):
                if g == 0:
                    w = wts[0][r]
                elif g == 2:
                    w = wts[1][r]
                else:
                    w = jnp.where(lane < 64, wts[0][r], wts[1][r])
                acc = acc + orecv[i, r, :, 128 * g : 128 * g + 128].astype(F32) * w
            out_ref[i, :, 128 * g : 128 * g + 128] = acc.astype(BF)
    s.drain()


def attention(q, kv, terms):
    seqs, count, keys = q.shape
    vals = kv.shape[2] - keys
    n = 2 * (1 + 6 * 3 + 8 + 6) + 6
    return pl.pallas_call(
        attention_kernel,
        name="attention",
        out_shape=(
            jax.ShapeDtypeStruct((seqs, count, vals), BF),
            jax.ShapeDtypeStruct(terms.shape[1:], F32),
        ),
        in_specs=[VSPEC] * 3,
        out_specs=(VSPEC, VSPEC),
        scratch_shapes=[
            VMEM((8, count, terms.shape[2]), BF),
            VMEM((seqs, 4, count, keys), BF),
            VMEM((seqs, 4, NZ, NC, count, keys + vals), BF),
            VMEM((seqs, 4, count, vals), BF),
            VMEM((seqs, 4, count, vals), BF),
            VMEM((seqs, 4, 8, count), F32),
            VMEM((seqs, 4, 8, count), F32),
            pltpu.SemaphoreType.DMA((n,)),
            pltpu.SemaphoreType.DMA((n,)),
        ],
        compiler_params=params(2, 40),
    )(q, kv, terms)


def tail_kernel(
    att_ref, tok_ref, cotx, ug_ref, ow, cw,
    block_out, out_ref, residual,
    terms, rt, blk, units, cots, taps, halo, st,
    send, recv, sums, r1, mid, r2, fin, zrecv, ss, rs,
):
    x, y, z, core = seq_pos()
    t, plus, minus = tensor_ring()
    me = lax.axis_index("seq")
    last = NX * NY * NZ * NC - 1
    rows, local = att_ref.shape
    half = rows // 2
    width = NT * local
    edge = CONV_DILATION
    total = 3 * width
    mine = total // 2
    tile = 256
    tiles = mine // tile
    per_tap = width // tile

    def pick(u, v):
        return jnp.where(core == 0, u, v)

    a, b = pick(x, y), pick(y, x)

    def along_a(k):
        return {"seq": pick(seq_dev(nxt(x, k), y, z, core), seq_dev(x, nxt(y, k), z, core))}

    def along_b(k):
        return {"seq": pick(seq_dev(x, nxt(y, k), z, core), seq_dev(nxt(x, k), y, z, core))}

    partner = {"seq": seq_dev(x, y, z, 1 - core)}
    zpeer = {"seq": seq_dev(x, y, 1 - z, core)}
    ap, am, bp, bm = along_a(1), along_a(3), along_b(1), along_b(3)
    opposite = {"tensor": nxt(t, 2)}
    after, before = seq_next(1), seq_prev()
    greet([plus, minus, opposite, partner, zpeer, ap, am, bp, bm, after, before])

    s = Sender(ss, rs)
    s.n = tiles

    def term(p, h):
        return terms.at[p, pl.ds(h * half, half)]

    def project_to(p):
        col = pl.multiple_of(p * local, 128)
        terms[p] = jnp.dot(
            att_ref[...], ow[:, pl.ds(col, local)], preferred_element_type=F32
        ).astype(BF)

    for k in (2, 1, 3, 0):
        project_to(nxt(t, k))
    red = Reduce4(s, term, lambda i, h: rt.at[i], t, plus, minus)
    red.begin()
    for j in range(3):
        cots[j] = cotx[:, (2 - j) * edge : (2 - j) * edge + half].reshape(rows, local)
    red.combine()
    parts = red.finish()
    for h in range(2):
        base = tok_ref[h * half : (h + 1) * half].astype(F32)
        blk[t, pl.ds(h * half, half)] = (parts[h] + base).astype(BF)
    g = Gather4(s, lambda p, h: blk.at[p, pl.ds(h * half, half)], t, plus, minus)
    g.begin()
    g.relay()
    g.wait_near()
    g.wait_far()

    averages, invs = [], []
    for h in range(2):
        at = slice(h * half, (h + 1) * half)
        values = jnp.concatenate([blk[i, at] for i in range(NT)], axis=1).astype(F32)
        average = jnp.mean(values, axis=-1, keepdims=True)
        centred = values - average
        inv = lax.rsqrt(jnp.mean(centred * centred, axis=-1, keepdims=True) + eps_norm)
        units[at] = gelu_exact(centred * inv).astype(BF)
        averages.append(average)
        invs.append(inv)

    def product(q):
        tap = lax.div(q, per_tap)
        col = pl.multiple_of(lax.rem(q, per_tap) * tile, tile)
        return lax.dot_general(
            units[:, pl.ds(col, tile)],
            cots[tap],
            (((0,), (0,)), ((), ())),
            preferred_element_type=F32,
        )

    def exchange(i):
        return pltpu.make_async_remote_copy(
            src_ref=send.at[i],
            dst_ref=recv.at[i],
            send_sem=ss.at[i],
            recv_sem=rs.at[i],
            device_id=partner,
            device_id_type=MESH,
        )

    @pl.loop(0, tiles)
    def _(i):
        send[i] = product((1 - core) * tiles + i).astype(BF)
        exchange(i).start()

    @pl.loop(0, tiles)
    def _(i):
        own = product(core * tiles + i)
        exchange(i).wait_recv()
        row = pl.multiple_of(i * tile, tile)
        sums[pl.ds(row, tile)] = (own + recv[i].astype(F32)).astype(BF)

    big = mine // 4
    small = big // 4
    bh = (0, big // 2)
    bn = (big // 2, big // 2)
    cut = (small // 2 + 15) // 16 * 16
    sh = (0, cut)
    sn = (cut, small - cut)

    def m16(v):
        return pl.multiple_of(v, 16)

    first = Reduce4(
        s,
        lambda p, h: sums.at[pl.ds(m16(p * big + bh[h]), bn[h])],
        lambda i, h: r1.at[i],
        a,
        ap,
        am,
    )
    first.begin()


    def tap(j):
        return jnp.dot(units[...], cw[j], preferred_element_type=F32).reshape(2, half, local)

    taps[0] = tap(0)
    up = s.go(taps.at[0, :, half - edge : half], halo.at[0], after)
    taps[2] = tap(2)
    down = s.go(taps.at[2, :, 0:edge], halo.at[1], before)
    lane = lax.broadcasted_iota(jnp.int32, (half, 128), 1)
    for h in range(2):
        at = pl.ds(h * half, half)
        n = (blk[t, at].astype(F32) - averages[h]) * invs[h]
        slope = ug_ref[h * half : (h + 1) * half] * gelu_slope(n)
        one = jnp.sum(slope, axis=-1, keepdims=True)
        two = jnp.sum(slope * n, axis=-1, keepdims=True)
        stats = jnp.where(lane == 0, one, jnp.where(lane == 1, two, 0.0))
        st[t, h] = stats.T[0:8]
    stat_copies = [s.go(st.at[t], st.at[t], d) for d in (plus, minus, opposite)]
    first.combine()
    taps[1] = tap(1)
    h0, h1 = first.finish()
    mid[0 : big // 2] = h0.astype(BF)
    mid[big // 2 : big] = h1.astype(BF)
    second = Reduce4(
        s,
        lambda p, h: mid.at[pl.ds(m16(p * small + sh[h]), sn[h])],
        lambda i, h: r2.at[i, pl.ds(0, sn[h])],
        b,
        bp,
        bm,
    )
    second.begin()
    up.wait_recv()
    down.wait_recv()
    second.combine()
    h0, h1 = second.finish()
    fin[0:cut] = h0.astype(BF)
    fin[cut:small] = h1.astype(BF)
    cz = s.go(fin, zrecv, zpeer)

    for h in range(2):
        own = blk[t, pl.ds(h * half, half)].astype(F32) + taps[1, h]
        left = jnp.where(me == 0, 0.0, halo[0, h])
        right = jnp.where(me == last, 0.0, halo[1, h])
        block_out[h, 0:edge] = (own[:edge] + left + taps[2, h, edge:half]).astype(BF)
        block_out[h, edge:half] = (own[edge:] + taps[0, h, 0 : half - edge] + right).astype(BF)

    cz.wait_recv()
    scale = (rows * NX * NY * NZ * NC) ** (-0.5)
    at = core * mine + a * big + b * small
    out_ref[pl.ds(m16(at), small)] = (
        (fin[...].astype(F32) + zrecv[...].astype(F32)) * scale
    ).astype(BF)
    g2 = Gather4(
        s,
        lambda p, h: out_ref.at[pl.ds(m16(core * mine + a * big + p * small + sh[h]), sn[h])],
        b,
        bp,
        bm,
    )
    g2.begin()
    g2.relay()
    g2.wait_near()
    g2.wait_far()

    def block(p):
        return out_ref.at[pl.ds(m16(core * mine + p * big), big)]

    g1 = Gather4(
        s,
        lambda p, h: out_ref.at[pl.ds(m16(core * mine + p * big + bh[h]), bn[h])],
        a,
        ap,
        am,
    )
    g1.begin()
    fw = [s.go(block(a), block(a), partner)]
    for c in stat_copies:
        c.wait_recv()
    for h in range(2):
        at = pl.ds(h * half, half)
        n = (blk[t, at].astype(F32) - averages[h]) * invs[h]
        slope = ug_ref[h * half : (h + 1) * half] * gelu_slope(n)
        both = (st[0, h] + st[1, h] + st[2, h] + st[3, h]) * (1.0 / width)
        wide = jnp.concatenate([both, jnp.zeros((120, 128), F32)], axis=0).T
        grad = (slope - wide[:, 0:1] - n * wide[:, 1:2]) * invs[h]
        residual[h] = (cotx[h, edge : edge + half].astype(F32) + grad).astype(BF)
    g1.relay()
    g1.wait_near()
    for k in (1, 3):
        fw.append(s.go(block(nxt(a, k)), block(nxt(a, k)), partner))
    g1.wait_far()
    fw.append(s.go(block(nxt(a, 2)), block(nxt(a, 2)), partner))
    for f in fw:
        f.wait_recv()
    s.drain()

    @pl.loop(0, tiles)
    def _(i):
        exchange(i).wait_send()


def tail(attended, tokens, cotx, unit_grad, out_weight, conv_weight):
    rows, local = attended.shape
    width = local * NT
    half = rows // 2
    edge = CONV_DILATION
    mine = 3 * width // 2
    big, small = mine // 4, mine // 16
    cut = (small // 2 + 15) // 16 * 16
    n = mine // 256 + 6 * 6 + 1 + 4 + 2 + 3
    return pl.pallas_call(
        tail_kernel,
        name="tail",
        out_shape=(
            jax.ShapeDtypeStruct((2, half, local), BF),
            jax.ShapeDtypeStruct((3 * width, local), BF),
            jax.ShapeDtypeStruct((2, half, local), BF),
        ),
        in_specs=[VSPEC] * 6,
        out_specs=(VSPEC,) * 3,
        scratch_shapes=[
            VMEM((NT, rows, local), BF),
            VMEM((8, half, local), BF),
            VMEM((NT, rows, local), BF),
            VMEM((rows, width), BF),
            VMEM((3, rows, local), BF),
            VMEM((3, 2, half, local), F32),
            VMEM((2, 2, edge, local), F32),
            VMEM((NT, 2, 8, 128), F32),
            VMEM((mine // 256, 256, local), BF),
            VMEM((mine // 256, 256, local), BF),
            VMEM((mine, local), BF),
            VMEM((8, big // 2, local), BF),
            VMEM((big, local), BF),
            VMEM((8, cut, local), BF),
            VMEM((small, local), BF),
            VMEM((small, local), BF),
            pltpu.SemaphoreType.DMA((n,)),
            pltpu.SemaphoreType.DMA((n,)),
        ],
        compiler_params=params(3, 40),
    )(attended, tokens, cotx, unit_grad, out_weight, conv_weight)


def body(tokens_in, query_weight, key_weight, value_weight, out_weight, conv_weight, cotangent):
    seqs, count, local = tokens_in.shape
    rows = seqs * count
    tokens = tokens_in.reshape(rows, local)
    q, kv, cotx, terms = project(
        tokens, cotangent, query_weight, key_weight, value_weight, conv_weight
    )
    attended, unit_grad = attention(q, kv, terms)
    block_out, conv_grad, residual_grad = tail(
        attended.reshape(rows, local), tokens, cotx, unit_grad, out_weight, conv_weight
    )
    return (block_out, conv_grad.reshape(3, local * NT, local), residual_grad)


def solution(mesh):
    placed = (
        P(None, "seq", "tensor"),
        P(None, "tensor"),
        P(None, "tensor"),
        P(None, "tensor"),
        P("tensor", None),
        P(None, None, "tensor"),
        P(None, "seq", "tensor"),
    )
    return jax.shard_map(
        body,
        mesh=mesh,
        in_specs=placed,
        out_specs=(P(None, "seq", "tensor"), P(None, None, "tensor"), P(None, "seq", "tensor")),
        check_vma=False,
    )
```

```python
import functools

import jax
import jax.numpy as jnp
from jax import lax
from jax.experimental import pallas as pl
from jax.experimental.pallas import tpu as pltpu
from jax.sharding import PartitionSpec as P

KEY = 64
VAL = 192
CONV_DILATION = 64
NT = 4
NX, NY, NZ, NC = 4, 4, 2, 2

eps_norm = 1e-05
root_half = 0.7071067811865476
inv_root_two_pi = 0.3989422804014327

MESH = pl.DeviceIdType.MESH
BF = jnp.bfloat16
F32 = jnp.float32
VMEM = pltpu.VMEM
VSPEC = pl.BlockSpec(memory_space=pltpu.VMEM)
HSPEC = pl.BlockSpec(memory_space=pltpu.HBM)


def normalize(values):
    average = jnp.mean(values, axis=-1, keepdims=True)
    centred = values - average
    inv_spread = lax.rsqrt(jnp.mean(centred * centred, axis=-1, keepdims=True) + eps_norm)
    return (centred * inv_spread, inv_spread)


def gelu_exact(values):
    return 0.5 * values * (1.0 + lax.erf(values * root_half))


def gelu_slope(values):
    return 0.5 * (1.0 + lax.erf(values * root_half)) + values * inv_root_two_pi * jnp.exp(
        -0.5 * values * values
    )


def seq_pos():
    s = lax.axis_index("seq")
    core = lax.rem(s, 2)
    z = lax.rem(lax.div(s, 2), 2)
    y = lax.rem(lax.div(s, 4), 4)
    x = lax.div(s, 16)
    return x, y, z, core


def seq_dev(x, y, z, core):
    return ((x * NY + y) * NZ + z) * NC + core


def nxt(i, k):
    return lax.rem(i + k, 4)


class Sender:
    def __init__(self, send_sems, recv_sems):
        self.ss, self.rs, self.n, self.flying = send_sems, recv_sems, 0, []

    def make(self, src, dst, dev):
        i = self.n
        self.n += 1
        return pltpu.make_async_remote_copy(
            src_ref=src,
            dst_ref=dst,
            send_sem=self.ss.at[i],
            recv_sem=self.rs.at[i],
            device_id=dev,
            device_id_type=MESH,
        )

    def go(self, src, dst, dev):
        c = self.make(src, dst, dev)
        c.start()
        self.flying.append(c)
        return c

    def drain(self):
        for c in self.flying:
            c.wait_send()
        self.flying = []


def greet(devs):
    barrier = pltpu.get_barrier_semaphore()
    for d in devs:
        pl.semaphore_signal(barrier, inc=1, device_id=d, device_id_type=MESH)
    pl.semaphore_wait(barrier, len(devs))


class Gather4:
    def __init__(self, sender, view, me, plus, minus, own=None):
        self.s, self.view, self.me, self.plus, self.minus = sender, view, me, plus, minus
        self.own = own or (lambda h: view(me, h))

    def begin(self):
        s, v, me, own = self.s, self.view, self.me, self.own
        self.c0 = s.go(own(0), v(me, 0), self.plus)
        self.c2 = s.go(own(1), v(me, 1), self.minus)
        self.c1 = s.go(own(1), v(me, 1), self.plus)
        self.c3 = s.go(own(0), v(me, 0), self.minus)

    def relay(self):
        s, v, me = self.s, self.view, self.me
        self.c0.wait_recv()
        self.c4 = s.go(v(nxt(me, 3), 0), v(nxt(me, 3), 0), self.plus)
        self.c2.wait_recv()
        self.c5 = s.go(v(nxt(me, 1), 1), v(nxt(me, 1), 1), self.minus)

    def wait_near(self):
        self.c1.wait_recv()
        self.c3.wait_recv()

    def wait_far(self):
        self.c4.wait_recv()
        self.c5.wait_recv()


class Reduce4:
    def __init__(self, sender, x, rbuf, me, plus, minus):
        self.s, self.x, self.r, self.me, self.plus, self.minus = sender, x, rbuf, me, plus, minus

    def begin(self):
        s, x, r, me = self.s, self.x, self.r, self.me
        self.a0 = s.go(x(nxt(me, 2), 0), r(0, 0), self.plus)
        self.a1 = s.go(x(nxt(me, 2), 1), r(1, 1), self.minus)
        self.b0 = s.go(x(nxt(me, 1), 1), r(2, 1), self.plus)
        self.b1 = s.go(x(nxt(me, 3), 0), r(3, 0), self.minus)

    def combine(self):
        s, x, r, me = self.s, self.x, self.r, self.me
        self.a0.wait_recv()
        t0 = r(6, 0)
        t0[...] = (x(nxt(me, 1), 0)[...].astype(F32) + r(0, 0)[...].astype(F32)).astype(BF)
        self.c0 = s.go(t0, r(4, 0), self.plus)
        self.a1.wait_recv()
        t1 = r(7, 1)
        t1[...] = (x(nxt(me, 3), 1)[...].astype(F32) + r(1, 1)[...].astype(F32)).astype(BF)
        self.c1 = s.go(t1, r(5, 1), self.minus)

    def finish(self):
        x, r, me = self.x, self.r, self.me
        self.b0.wait_recv()
        self.b1.wait_recv()
        self.c0.wait_recv()
        h0 = x(me, 0)[...].astype(F32) + r(3, 0)[...].astype(F32) + r(4, 0)[...].astype(F32)
        self.c1.wait_recv()
        h1 = x(me, 1)[...].astype(F32) + r(2, 1)[...].astype(F32) + r(5, 1)[...].astype(F32)
        return h0, h1


def tensor_ring():
    t = lax.axis_index("tensor")
    return t, {"tensor": nxt(t, 1)}, {"tensor": nxt(t, 3)}


def params(cid, mib):
    return pltpu.CompilerParams(
        collective_id=cid, has_side_effects=True, vmem_limit_bytes=mib * 1024 * 1024
    )


def seq_next(k):
    return {"seq": lax.rem(lax.axis_index("seq") + k, NX * NY * NZ * NC)}


def seq_prev():
    return seq_next(NX * NY * NZ * NC - 1)


def fetch(sem, i, src, dst):
    c = pltpu.make_async_copy(src, dst, sem.at[i])
    c.start()
    return c


def front_kernel(
    tok_hbm, cot_hbm, wq_hbm, wk_hbm, wv_hbm, ow_hbm, cw_hbm,
    att, full, cotx, terms_ref, owg,
    wq, wk, wv, cw, cots, qbuf, kvbuf, obuf, orecv, lbuf, lrecv, ss, rs, ls,
):
    x, y, z, core = seq_pos()
    t, plus, minus = tensor_ring()
    opposite = {"tensor": nxt(t, 2)}
    seqs, count, width = tok_hbm.shape
    rows = seqs * count
    half = count // 2
    edge = CONV_DILATION
    me = lax.axis_index("seq")
    last = NX * NY * NZ * NC - 1
    s = Sender(ss, rs)

    ltok = fetch(ls, 0, tok_hbm, full.at[t])
    lcot = fetch(ls, 1, cot_hbm, cotx.at[:, edge : edge + count])
    lcw = fetch(ls, 2, cw_hbm, cw)
    lws = [fetch(ls, 3, wq_hbm, wq), fetch(ls, 4, wk_hbm, wk), fetch(ls, 5, wv_hbm, wv)]
    partner = {"seq": seq_dev(x, y, z, 1 - core)}
    zpeer = {"seq": seq_dev(x, y, 1 - z, core)}
    xs = [{"seq": seq_dev(nxt(x, k), y, z, core)} for k in (1, 2, 3)]
    ys = [{"seq": seq_dev(x, nxt(y, k), z, core)} for k in (1, 2, 3)]
    axes = ((x, xs, y, ys), (y, ys, x, xs))
    greet([plus, minus, opposite, seq_next(1), seq_prev(), partner, zpeer] + xs + ys)

    def token_ring(i):
        return Gather4(
            s,
            lambda slot, h: full.at[slot, i, pl.ds(h * half, half)],
            t,
            plus,
            minus,
            own=lambda h: tok_hbm.at[i, pl.ds(h * half, half)],
        )

    def weight_gather():
        srows = ow_hbm.shape[0] // 8
        scols = ow_hbm.shape[1] // 4

        def pick(u, v):
            return jnp.where(core == 0, u, v)

        a, b = pick(x, y), pick(y, x)

        def dev(u, v):
            return {"seq": pick(u["seq"], v["seq"])}

        def rows_of(p):
            return pl.ds(pl.multiple_of((core * 4 + p) * srows, 16), srows)

        def cols_of(p):
            return pl.ds(pl.multiple_of(p * scols, 128), scols)

        zc = []
        for k, d in ((1, minus), (3, plus), (2, opposite)):
            piece = (rows_of(a), cols_of(b))
            zc.append(s.go(ow_hbm.at[piece], owg.at[(k - 1,) + piece], d))
        yield
        for c in zc:
            c.wait_recv()
        cut = (0, 32, srows)

        def view2(p, h):
            at = pl.multiple_of((core * 4 + a) * srows + cut[h], 16)
            return owg.at[:, pl.ds(at, cut[h + 1] - cut[h]), cols_of(p)]

        g2 = Gather4(s, view2, b, dev(ys[0], xs[0]), dev(ys[2], xs[2]))
        g2.begin()
        yield
        g2.relay()
        yield
        g2.wait_near()
        g2.wait_far()
        yield
        wide = ow_hbm.shape[1] // 2
        g1 = Gather4(
            s,
            lambda p, h: owg.at[:, rows_of(p), pl.ds(h * wide, wide)],
            a,
            dev(xs[0], ys[0]),
            dev(xs[2], ys[2]),
        )
        g1.begin()
        fw = []

        def forward(p):
            ref = owg.at[:, rows_of(p)]
            fw.append(s.go(ref, ref, partner))

        forward(a)
        yield
        g1.relay()
        yield
        g1.wait_near()
        forward(nxt(a, 1))
        forward(nxt(a, 3))
        yield
        g1.wait_far()
        forward(nxt(a, 2))
        yield
        for f in fw:
            f.wait_recv()

    def exchange(i):
        a, a_dev, b, b_dev = axes[i]
        own = kvbuf.at[i, a, z, core]
        cz = s.go(own, own, zpeer)

        def ring(zz):
            return Gather4(
                s,
                lambda slot, h: kvbuf.at[i, slot, zz, core, pl.ds(h * half, half)],
                a,
                a_dev[0],
                a_dev[2],
            )

        gk, go = ring(z), ring(1 - z)
        gq = Gather4(
            s, lambda slot, h: qbuf.at[i, slot, pl.ds(h * half, half)], b, b_dev[0], b_dev[2]
        )
        gk.begin()
        gq.begin()
        fw = []

        def forward(p, zz):
            ref = kvbuf.at[i, p, zz, core]
            fw.append(s.go(ref, ref, partner))

        forward(a, z)
        yield
        gk.relay()
        gq.relay()
        yield
        cz.wait_recv()
        go.begin()
        forward(a, 1 - z)
        yield
        gk.wait_near()
        forward(nxt(a, 1), z)
        forward(nxt(a, 3), z)
        yield
        gk.wait_far()
        forward(nxt(a, 2), z)
        go.relay()
        yield
        go.wait_near()
        forward(nxt(a, 1), 1 - z)
        forward(nxt(a, 3), 1 - z)
        yield
        go.wait_far()
        forward(nxt(a, 2), 1 - z)
        gq.wait_near()
        gq.wait_far()
        yield
        for f in fw:
            f.wait_recv()

    def project(i):
        a, _, b, _ = axes[i]
        values = jnp.concatenate([full[p, i] for p in range(NT)], axis=1).astype(F32)
        hidden = normalize(values)[0].astype(BF)
        qbuf[i, b] = jnp.dot(hidden, wq[...], preferred_element_type=F32).astype(BF)
        keys = wk.shape[1]
        kvbuf[i, a, z, core, :, 0:keys] = jnp.dot(
            hidden, wk[...], preferred_element_type=F32
        ).astype(BF)
        kvbuf[i, a, z, core, :, keys:] = jnp.dot(
            hidden, wv[...], preferred_element_type=F32
        ).astype(BF)

    def term(p):
        acc = jnp.zeros((rows, width), F32)
        for j in range(3):
            acc = acc + lax.dot_general(
                cots[j],
                cw[j, p * width : (p + 1) * width],
                (((1,), (1,)), ((), ())),
                preferred_element_type=F32,
            )
        terms_ref[p] = acc.astype(BF)

    keys = NX * NZ * NC * count
    lane2 = lax.broadcasted_iota(jnp.int32, (2 * count, 128), 1)
    lane = lax.broadcasted_iota(jnp.int32, (count, 128), 1)

    def attend(i, ks):
        b = axes[i][2]
        r0, r1 = nxt(b, ks[0]), nxt(b, ks[1])
        q = jnp.concatenate([qbuf[i, r0], qbuf[i, r1]], axis=0)
        q = (q.astype(F32) * KEY ** (-0.5)).astype(BF)
        k = kvbuf[i, :, :, :, :, 0:128].reshape(keys, 128)
        parts = []
        stats = jnp.zeros((2 * count, 128), F32)
        for h in range(2):
            qh = jnp.where((lane2 < KEY) if h == 0 else (lane2 >= KEY), q, jnp.zeros_like(q))
            sc = lax.dot_general(qh, k, (((1,), (1,)), ((), ())), preferred_element_type=F32)
            top = jnp.max(sc, axis=-1, keepdims=True)
            w = jnp.exp(sc - top)
            total = jnp.sum(w, axis=-1, keepdims=True)
            v = kvbuf[i, :, :, :, :, 128 + 128 * h : 384 + 128 * h].reshape(keys, 256)
            acc = jnp.dot(w.astype(BF), v, preferred_element_type=F32) / total
            parts.append(acc)
            stats = jnp.where(lane2 == h, top + jnp.log(total), stats)
        mid = jnp.where(lane2 < 64, parts[0][:, 128:], parts[1][:, :128])
        for n, r in enumerate((r0, r1)):
            at = slice(n * count, (n + 1) * count)
            obuf[i, r, :, 0:128] = parts[0][at, :128].astype(BF)
            obuf[i, r, :, 128:256] = mid[at].astype(BF)
            obuf[i, r, :, 256:384] = parts[1][at, 128:].astype(BF)
            lbuf[i, r] = stats[at].T[0:8]

    osent = [[], []]

    def send_out(i, k):
        b, b_dev = axes[i][2], axes[i][3]
        dev = b_dev[k - 1]
        osent[i].append(s.go(obuf.at[i, nxt(b, k)], orecv.at[i, b], dev))
        osent[i].append(s.go(lbuf.at[i, nxt(b, k)], lrecv.at[i, b], dev))

    def combine(i):
        b = axes[i][2]
        orecv[i, b] = obuf[i, b]
        lrecv[i, b] = lbuf[i, b]
        for c in osent[i]:
            c.wait_recv()
        logs = []
        for r in range(4):
            wide = jnp.concatenate([lrecv[i, r], jnp.zeros((120, 128), F32)], axis=0).T
            logs.append([wide[:, h : h + 1] for h in range(2)])
        wts = []
        for h in range(2):
            top = logs[0][h]
            for r in range(1, 4):
                top = jnp.maximum(top, logs[r][h])
            e = [jnp.exp(logs[r][h] - top) for r in range(4)]
            total = e[0] + e[1] + e[2] + e[3]
            wts.append([er / total for er in e])
        for g in range(3):
            acc = jnp.zeros((count, 128), F32)
            for r in range(4):
                if g == 0:
                    w = wts[0][r]
                elif g == 2:
                    w = wts[1][r]
                else:
                    w = jnp.where(lane < 64, wts[0][r], wts[1][r])
                acc = acc + orecv[i, r, :, 128 * g : 128 * g + 128].astype(F32) * w
            att[t, i, :, 128 * g : 128 * g + 128] = acc.astype(BF)
        ring = Gather4(
            s, lambda slot, h: att.at[slot, i, pl.ds(h * half, half)], t, plus, minus
        )
        ring.begin()
        return ring

    def step(gen):
        next(gen, None)

    tok0, tok1 = token_ring(0), token_ring(1)
    tok0.begin()
    up = s.go(cot_hbm.at[:, count - edge : count], cotx.at[:, 0:edge], seq_next(1))
    down = s.go(cot_hbm.at[:, 0:edge], cotx.at[:, edge + count : 2 * edge + count], seq_prev())
    lcot.wait()
    up.wait_recv()
    down.wait_recv()

    @pl.when(me == 0)
    def _():
        cotx[:, 0:edge] = jnp.zeros((2, edge, width), BF)

    @pl.when(me == last)
    def _():
        cotx[:, edge + count : 2 * edge + count] = jnp.zeros((2, edge, width), BF)

    for j in range(3):
        cots[j] = cotx[:, (2 - j) * edge : (2 - j) * edge + count].reshape(rows, width)
    lcw.wait()
    term(0)
    tok0.relay()
    weights = weight_gather()
    step(weights)
    tok1.begin()
    for p in range(1, NT):
        term(p)
    ltok.wait()
    for c in lws:
        c.wait()
    tok0.wait_near()
    tok0.wait_far()
    project(0)
    ex0 = exchange(0)
    step(ex0)
    tok1.relay()
    step(weights)
    step(ex0)
    step(ex0)
    step(weights)
    tok1.wait_near()
    tok1.wait_far()
    project(1)
    ex1 = exchange(1)
    step(ex1)
    step(weights)
    step(ex0)
    step(ex0)
    step(ex1)
    step(ex0)
    step(ex1)
    step(ex0)
    step(ex0)
    attend(0, (2, 1))
    send_out(0, 2)
    send_out(0, 1)
    step(ex1)
    step(ex1)
    step(weights)
    attend(0, (3, 0))
    send_out(0, 3)
    step(ex1)
    step(ex1)
    step(weights)
    step(ex1)
    attend(1, (2, 1))
    send_out(1, 2)
    send_out(1, 1)
    ring0 = combine(0)
    step(weights)
    attend(1, (3, 0))
    send_out(1, 3)
    ring0.relay()
    step(weights)
    ring1 = combine(1)
    step(weights)
    ring1.relay()
    ring0.wait_near()
    ring0.wait_far()
    ring1.wait_near()
    ring1.wait_far()
    for gen in (ex0, ex1, weights):
        for _ in gen:
            pass
    s.drain()


def in_hbm(v):
    return pltpu.with_memory_space_constraint(v, pltpu.HBM)


def front(tokens, cot, wq, wk, wv, ow, cw):
    seqs, count, width = tokens.shape
    keys, vals = wk.shape[1], wv.shape[1]
    n = 12 + 2 + 3 + 16 + 2 * 27 + 12 + 12
    return pl.pallas_call(
        front_kernel,
        name="front",
        out_shape=(
            jax.ShapeDtypeStruct((NT, seqs, count, vals), BF),
            jax.ShapeDtypeStruct((NT, seqs, count, width), BF),
            jax.ShapeDtypeStruct((seqs, count + 2 * CONV_DILATION, width), BF),
            jax.ShapeDtypeStruct((NT, seqs * count, width), BF),
            jax.ShapeDtypeStruct((NT - 1,) + ow.shape, BF),
        ),
        in_specs=[HSPEC] * 7,
        out_specs=(VSPEC,) * 5,
        scratch_shapes=[
            VMEM(wq.shape, BF),
            VMEM(wk.shape, BF),
            VMEM(wv.shape, BF),
            VMEM(cw.shape, BF),
            VMEM((3, seqs * count, width), BF),
            VMEM((seqs, 4, count, keys), BF),
            VMEM((seqs, 4, NZ, NC, count, keys + vals), BF),
            VMEM((seqs, 4, count, vals), BF),
            VMEM((seqs, 4, count, vals), BF),
            VMEM((seqs, 4, 8, count), F32),
            VMEM((seqs, 4, 8, count), F32),
            pltpu.SemaphoreType.DMA((n,)),
            pltpu.SemaphoreType.DMA((n,)),
            pltpu.SemaphoreType.DMA((6,)),
        ],
        compiler_params=params(1, 28),
    )(*[in_hbm(v) for v in (tokens, cot, wq, wk, wv, ow, cw)])


def tail_kernel(
    att, full, cotx, terms, ow, owg, cw,
    block_out, out_ref, residual,
    ug_ref, rt, blk, units, cots, taps, halo, st,
    send, recv, sums, r1, mid, r2, fin, zrecv, ss, rs,
):
    x, y, z, core = seq_pos()
    t, plus, minus = tensor_ring()
    me = lax.axis_index("seq")
    last = NX * NY * NZ * NC - 1
    rows, local = terms.shape[1:]
    half = rows // 2
    width = NT * local
    edge = CONV_DILATION
    total = 3 * width
    mine = total // 2
    tile = 256
    tiles = mine // tile
    per_tap = width // tile

    def pick(u, v):
        return jnp.where(core == 0, u, v)

    a, b = pick(x, y), pick(y, x)

    def along_a(k):
        return {"seq": pick(seq_dev(nxt(x, k), y, z, core), seq_dev(x, nxt(y, k), z, core))}

    def along_b(k):
        return {"seq": pick(seq_dev(x, nxt(y, k), z, core), seq_dev(nxt(x, k), y, z, core))}

    partner = {"seq": seq_dev(x, y, z, 1 - core)}
    zpeer = {"seq": seq_dev(x, y, 1 - z, core)}
    ap, am, bp, bm = along_a(1), along_a(3), along_b(1), along_b(3)
    opposite = {"tensor": nxt(t, 2)}
    after, before = seq_next(1), seq_prev()
    greet([plus, minus, opposite, partner, zpeer, ap, am, bp, bm, after, before])

    s = Sender(ss, rs)
    s.n = tiles

    red = Reduce4(
        s,
        lambda p, h: terms.at[p, pl.ds(h * half, half)],
        lambda i, h: rt.at[i],
        t,
        plus,
        minus,
    )
    red.begin()
    for j in range(3):
        cots[j] = cotx[:, (2 - j) * edge : (2 - j) * edge + half].reshape(rows, local)
    averages, invs = [], []
    for h in range(2):
        at = slice(h * half, (h + 1) * half)
        mixed = jnp.dot(att[t, h], ow[...], preferred_element_type=F32)
        for k in range(1, NT):
            mixed = mixed + jnp.dot(att[nxt(t, k), h], owg[k - 1], preferred_element_type=F32)
        for p in range(NT):
            blk[p, at] = (
                mixed[:, p * local : (p + 1) * local] + full[p, h].astype(F32)
            ).astype(BF)
        values = jnp.concatenate([blk[i, at] for i in range(NT)], axis=1).astype(F32)
        average = jnp.mean(values, axis=-1, keepdims=True)
        centred = values - average
        inv = lax.rsqrt(jnp.mean(centred * centred, axis=-1, keepdims=True) + eps_norm)
        units[at] = gelu_exact(centred * inv).astype(BF)
        averages.append(average)
        invs.append(inv)
    red.combine()

    def product(q):
        tap = lax.div(q, per_tap)
        col = pl.multiple_of(lax.rem(q, per_tap) * tile, tile)
        return lax.dot_general(
            units[:, pl.ds(col, tile)],
            cots[tap],
            (((0,), (0,)), ((), ())),
            preferred_element_type=F32,
        )

    def exchange(i):
        return pltpu.make_async_remote_copy(
            src_ref=send.at[i],
            dst_ref=recv.at[i],
            send_sem=ss.at[i],
            recv_sem=rs.at[i],
            device_id=partner,
            device_id_type=MESH,
        )

    @pl.loop(0, tiles)
    def _(i):
        send[i] = product((1 - core) * tiles + i).astype(BF)
        exchange(i).start()

    @pl.loop(0, tiles)
    def _(i):
        own = product(core * tiles + i)
        exchange(i).wait_recv()
        row = pl.multiple_of(i * tile, tile)
        sums[pl.ds(row, tile)] = (own + recv[i].astype(F32)).astype(BF)

    big = mine // 4
    small = big // 4
    bh = (0, big // 2)
    bn = (big // 2, big // 2)
    cut = (small // 2 + 15) // 16 * 16
    sh = (0, cut)
    sn = (cut, small - cut)

    def m16(v):
        return pl.multiple_of(v, 16)

    first = Reduce4(
        s,
        lambda p, h: sums.at[pl.ds(m16(p * big + bh[h]), bn[h])],
        lambda i, h: r1.at[i],
        a,
        ap,
        am,
    )
    first.begin()


    def tap(j):
        return jnp.dot(units[...], cw[j], preferred_element_type=F32).reshape(2, half, local)

    taps[0] = tap(0)
    up = s.go(taps.at[0, :, half - edge : half], halo.at[0], after)
    taps[2] = tap(2)
    down = s.go(taps.at[2, :, 0:edge], halo.at[1], before)
    first.combine()
    taps[1] = tap(1)
    h0, h1 = first.finish()
    mid[0 : big // 2] = h0.astype(BF)
    mid[big // 2 : big] = h1.astype(BF)
    second = Reduce4(
        s,
        lambda p, h: mid.at[pl.ds(m16(p * small + sh[h]), sn[h])],
        lambda i, h: r2.at[i, pl.ds(0, sn[h])],
        b,
        bp,
        bm,
    )
    second.begin()
    parts = red.finish()
    for h in range(2):
        ug_ref[h * half : (h + 1) * half] = parts[h]
    lane = lax.broadcasted_iota(jnp.int32, (half, 128), 1)
    for h in range(2):
        at = pl.ds(h * half, half)
        n = (blk[t, at].astype(F32) - averages[h]) * invs[h]
        slope = ug_ref[h * half : (h + 1) * half] * gelu_slope(n)
        one = jnp.sum(slope, axis=-1, keepdims=True)
        two = jnp.sum(slope * n, axis=-1, keepdims=True)
        stats = jnp.where(lane == 0, one, jnp.where(lane == 1, two, 0.0))
        st[t, h] = stats.T[0:8]
    stat_copies = [s.go(st.at[t], st.at[t], d) for d in (plus, minus, opposite)]
    second.combine()
    h0, h1 = second.finish()
    fin[0:cut] = h0.astype(BF)
    fin[cut:small] = h1.astype(BF)
    cz = s.go(fin, zrecv, zpeer)
    up.wait_recv()
    down.wait_recv()

    for h in range(2):
        own = blk[t, pl.ds(h * half, half)].astype(F32) + taps[1, h]
        left = jnp.where(me == 0, 0.0, halo[0, h])
        right = jnp.where(me == last, 0.0, halo[1, h])
        block_out[h, 0:edge] = (own[:edge] + left + taps[2, h, edge:half]).astype(BF)
        block_out[h, edge:half] = (own[edge:] + taps[0, h, 0 : half - edge] + right).astype(BF)

    cz.wait_recv()
    scale = (rows * NX * NY * NZ * NC) ** (-0.5)
    at = core * mine + a * big + b * small
    out_ref[pl.ds(m16(at), small)] = (
        (fin[...].astype(F32) + zrecv[...].astype(F32)) * scale
    ).astype(BF)
    g2 = Gather4(
        s,
        lambda p, h: out_ref.at[pl.ds(m16(core * mine + a * big + p * small + sh[h]), sn[h])],
        b,
        bp,
        bm,
    )
    g2.begin()
    g2.relay()
    g2.wait_near()
    g2.wait_far()

    def block(p):
        return out_ref.at[pl.ds(m16(core * mine + p * big), big)]

    g1 = Gather4(
        s,
        lambda p, h: out_ref.at[pl.ds(m16(core * mine + p * big + bh[h]), bn[h])],
        a,
        ap,
        am,
    )
    g1.begin()
    fw = [s.go(block(a), block(a), partner)]
    for c in stat_copies:
        c.wait_recv()
    for h in range(2):
        at = pl.ds(h * half, half)
        n = (blk[t, at].astype(F32) - averages[h]) * invs[h]
        slope = ug_ref[h * half : (h + 1) * half] * gelu_slope(n)
        both = (st[0, h] + st[1, h] + st[2, h] + st[3, h]) * (1.0 / width)
        wide = jnp.concatenate([both, jnp.zeros((120, 128), F32)], axis=0).T
        grad = (slope - wide[:, 0:1] - n * wide[:, 1:2]) * invs[h]
        residual[h] = (cotx[h, edge : edge + half].astype(F32) + grad).astype(BF)
    g1.relay()
    g1.wait_near()
    for k in (1, 3):
        fw.append(s.go(block(nxt(a, k)), block(nxt(a, k)), partner))
    g1.wait_far()
    fw.append(s.go(block(nxt(a, 2)), block(nxt(a, 2)), partner))
    for f in fw:
        f.wait_recv()
    s.drain()

    @pl.loop(0, tiles)
    def _(i):
        exchange(i).wait_send()


def tail(attended, full, cotx, terms, out_weight, others, conv_weight):
    _, rows, local = terms.shape
    width = local * NT
    half = rows // 2
    edge = CONV_DILATION
    mine = 3 * width // 2
    big, small = mine // 4, mine // 16
    cut = (small // 2 + 15) // 16 * 16
    n = mine // 256 + 6 * 5 + 1 + 4 + 2 + 3
    return pl.pallas_call(
        tail_kernel,
        name="tail",
        out_shape=(
            jax.ShapeDtypeStruct((2, half, local), BF),
            jax.ShapeDtypeStruct((3 * width, local), BF),
            jax.ShapeDtypeStruct((2, half, local), BF),
        ),
        in_specs=[VSPEC] * 7,
        out_specs=(VSPEC,) * 3,
        scratch_shapes=[
            VMEM((rows, local), F32),
            VMEM((8, half, local), BF),
            VMEM((NT, rows, local), BF),
            VMEM((rows, width), BF),
            VMEM((3, rows, local), BF),
            VMEM((3, 2, half, local), F32),
            VMEM((2, 2, edge, local), F32),
            VMEM((NT, 2, 8, 128), F32),
            VMEM((mine // 256, 256, local), BF),
            VMEM((mine // 256, 256, local), BF),
            VMEM((mine, local), BF),
            VMEM((8, big // 2, local), BF),
            VMEM((big, local), BF),
            VMEM((8, cut, local), BF),
            VMEM((small, local), BF),
            VMEM((small, local), BF),
            pltpu.SemaphoreType.DMA((n,)),
            pltpu.SemaphoreType.DMA((n,)),
        ],
        compiler_params=params(3, 24),
    )(attended, full, cotx, terms, out_weight, others, conv_weight)


def body(tokens_in, query_weight, key_weight, value_weight, out_weight, conv_weight, cotangent):
    local = tokens_in.shape[2]
    attended, full, cotx, terms, others = front(
        tokens_in, cotangent, query_weight, key_weight, value_weight, out_weight, conv_weight
    )
    block_out, conv_grad, residual_grad = tail(
        attended, full, cotx, terms, out_weight, others, conv_weight
    )
    return (block_out, conv_grad.reshape(3, local * NT, local), residual_grad)


def solution(mesh):
    placed = (
        P(None, "seq", "tensor"),
        P(None, "tensor"),
        P(None, "tensor"),
        P(None, "tensor"),
        P("tensor", None),
        P(None, None, "tensor"),
        P(None, "seq", "tensor"),
    )
    return jax.shard_map(
        body,
        mesh=mesh,
        in_specs=placed,
        out_specs=(P(None, "seq", "tensor"), P(None, None, "tensor"), P(None, "seq", "tensor")),
        check_vma=False,
    )
```

```python
import functools

import jax
import jax.numpy as jnp
from jax import lax
from jax.experimental import pallas as pl
from jax.experimental.pallas import tpu as pltpu
from jax.sharding import PartitionSpec as P

KEY = 64
VAL = 192
CONV_DILATION = 64
NT = 4
NX, NY, NZ, NC = 4, 4, 2, 2

eps_norm = 1e-05
root_half = 0.7071067811865476
inv_root_two_pi = 0.3989422804014327

MESH = pl.DeviceIdType.MESH
BF = jnp.bfloat16
F32 = jnp.float32
VMEM = pltpu.VMEM
VSPEC = pl.BlockSpec(memory_space=pltpu.VMEM)
HSPEC = pl.BlockSpec(memory_space=pltpu.HBM)


def normalize(values):
    average = jnp.mean(values, axis=-1, keepdims=True)
    centred = values - average
    inv_spread = lax.rsqrt(jnp.mean(centred * centred, axis=-1, keepdims=True) + eps_norm)
    return (centred * inv_spread, inv_spread)


def gelu_exact(values):
    return 0.5 * values * (1.0 + lax.erf(values * root_half))


def gelu_slope(values):
    return 0.5 * (1.0 + lax.erf(values * root_half)) + values * inv_root_two_pi * jnp.exp(
        -0.5 * values * values
    )


def seq_pos():
    s = lax.axis_index("seq")
    core = lax.rem(s, 2)
    z = lax.rem(lax.div(s, 2), 2)
    y = lax.rem(lax.div(s, 4), 4)
    x = lax.div(s, 16)
    return x, y, z, core


def seq_dev(x, y, z, core):
    return ((x * NY + y) * NZ + z) * NC + core


def nxt(i, k):
    return lax.rem(i + k, 4)


class Sender:
    def __init__(self, send_sems, recv_sems):
        self.ss, self.rs, self.n, self.flying = send_sems, recv_sems, 0, []

    def make(self, src, dst, dev):
        i = self.n
        self.n += 1
        return pltpu.make_async_remote_copy(
            src_ref=src,
            dst_ref=dst,
            send_sem=self.ss.at[i],
            recv_sem=self.rs.at[i],
            device_id=dev,
            device_id_type=MESH,
        )

    def go(self, src, dst, dev):
        c = self.make(src, dst, dev)
        c.start()
        self.flying.append(c)
        return c

    def drain(self):
        for c in self.flying:
            c.wait_send()
        self.flying = []


def greet(devs):
    barrier = pltpu.get_barrier_semaphore()
    for d in devs:
        pl.semaphore_signal(barrier, inc=1, device_id=d, device_id_type=MESH)
    pl.semaphore_wait(barrier, len(devs))


class Gather4:
    def __init__(self, sender, view, me, plus, minus, own=None):
        self.s, self.view, self.me, self.plus, self.minus = sender, view, me, plus, minus
        self.own = own or (lambda h: view(me, h))

    def begin(self):
        s, v, me, own = self.s, self.view, self.me, self.own
        self.c0 = s.go(own(0), v(me, 0), self.plus)
        self.c2 = s.go(own(1), v(me, 1), self.minus)
        self.c1 = s.go(own(1), v(me, 1), self.plus)
        self.c3 = s.go(own(0), v(me, 0), self.minus)

    def relay(self):
        s, v, me = self.s, self.view, self.me
        self.c0.wait_recv()
        self.c4 = s.go(v(nxt(me, 3), 0), v(nxt(me, 3), 0), self.plus)
        self.c2.wait_recv()
        self.c5 = s.go(v(nxt(me, 1), 1), v(nxt(me, 1), 1), self.minus)

    def wait_near(self):
        self.c1.wait_recv()
        self.c3.wait_recv()

    def wait_far(self):
        self.c4.wait_recv()
        self.c5.wait_recv()


class Reduce4:
    def __init__(self, sender, x, rbuf, me, plus, minus):
        self.s, self.x, self.r, self.me, self.plus, self.minus = sender, x, rbuf, me, plus, minus

    def begin(self):
        s, x, r, me = self.s, self.x, self.r, self.me
        self.a0 = s.go(x(nxt(me, 2), 0), r(0, 0), self.plus)
        self.a1 = s.go(x(nxt(me, 2), 1), r(1, 1), self.minus)
        self.b0 = s.go(x(nxt(me, 1), 1), r(2, 1), self.plus)
        self.b1 = s.go(x(nxt(me, 3), 0), r(3, 0), self.minus)

    def combine(self):
        s, x, r, me = self.s, self.x, self.r, self.me
        self.a0.wait_recv()
        t0 = r(6, 0)
        t0[...] = (x(nxt(me, 1), 0)[...].astype(F32) + r(0, 0)[...].astype(F32)).astype(BF)
        self.c0 = s.go(t0, r(4, 0), self.plus)
        self.a1.wait_recv()
        t1 = r(7, 1)
        t1[...] = (x(nxt(me, 3), 1)[...].astype(F32) + r(1, 1)[...].astype(F32)).astype(BF)
        self.c1 = s.go(t1, r(5, 1), self.minus)

    def finish(self):
        x, r, me = self.x, self.r, self.me
        self.b0.wait_recv()
        self.b1.wait_recv()
        self.c0.wait_recv()
        h0 = x(me, 0)[...].astype(F32) + r(3, 0)[...].astype(F32) + r(4, 0)[...].astype(F32)
        self.c1.wait_recv()
        h1 = x(me, 1)[...].astype(F32) + r(2, 1)[...].astype(F32) + r(5, 1)[...].astype(F32)
        return h0, h1


def tensor_ring():
    t = lax.axis_index("tensor")
    return t, {"tensor": nxt(t, 1)}, {"tensor": nxt(t, 3)}


def params(cid, mib):
    return pltpu.CompilerParams(
        collective_id=cid, has_side_effects=True, vmem_limit_bytes=mib * 1024 * 1024
    )


def seq_next(k):
    return {"seq": lax.rem(lax.axis_index("seq") + k, NX * NY * NZ * NC)}


def seq_prev():
    return seq_next(NX * NY * NZ * NC - 1)


def fetch(sem, i, src, dst):
    c = pltpu.make_async_copy(src, dst, sem.at[i])
    c.start()
    return c


def front_kernel(
    tok_hbm, cot_hbm, wq_hbm, wk_hbm, wv_hbm, ow_hbm, cw_hbm,
    att, full, cotx, terms_ref, owg,
    wq, wk, wv, cw, cots, qbuf, kvbuf, obuf, orecv, lbuf, lrecv, ss, rs, ls,
):
    x, y, z, core = seq_pos()
    t, plus, minus = tensor_ring()
    opposite = {"tensor": nxt(t, 2)}
    seqs, count, width = tok_hbm.shape
    rows = seqs * count
    half = count // 2
    edge = CONV_DILATION
    me = lax.axis_index("seq")
    last = NX * NY * NZ * NC - 1
    s = Sender(ss, rs)

    ltok = fetch(ls, 0, tok_hbm, full.at[t])
    lcot = fetch(ls, 1, cot_hbm, cotx.at[:, edge : edge + count])
    lcw = fetch(ls, 2, cw_hbm, cw)
    lws = [fetch(ls, 3, wq_hbm, wq), fetch(ls, 4, wk_hbm, wk), fetch(ls, 5, wv_hbm, wv)]
    partner = {"seq": seq_dev(x, y, z, 1 - core)}
    zpeer = {"seq": seq_dev(x, y, 1 - z, core)}
    xs = [{"seq": seq_dev(nxt(x, k), y, z, core)} for k in (1, 2, 3)]
    ys = [{"seq": seq_dev(x, nxt(y, k), z, core)} for k in (1, 2, 3)]
    axes = ((x, xs, y, ys), (y, ys, x, xs))
    greet([plus, minus, opposite, seq_next(1), seq_prev(), partner, zpeer] + xs + ys)

    def token_ring(i):
        return Gather4(
            s,
            lambda slot, h: full.at[slot, i, pl.ds(h * half, half)],
            t,
            plus,
            minus,
            own=lambda h: tok_hbm.at[i, pl.ds(h * half, half)],
        )

    def weight_gather():
        srows = ow_hbm.shape[0] // 8
        scols = ow_hbm.shape[1] // 4

        def pick(u, v):
            return jnp.where(core == 0, u, v)

        a, b = pick(x, y), pick(y, x)

        def dev(u, v):
            return {"seq": pick(u["seq"], v["seq"])}

        def rows_of(p):
            return pl.ds(pl.multiple_of((core * 4 + p) * srows, 16), srows)

        def cols_of(p):
            return pl.ds(pl.multiple_of(p * scols, 128), scols)

        zc = []
        for k, d in ((1, minus), (3, plus), (2, opposite)):
            piece = (rows_of(a), cols_of(b))
            zc.append(s.go(ow_hbm.at[piece], owg.at[(k - 1,) + piece], d))
        yield
        for c in zc:
            c.wait_recv()
        cut = (0, 32, srows)

        def view2(p, h):
            at = pl.multiple_of((core * 4 + a) * srows + cut[h], 16)
            return owg.at[:, pl.ds(at, cut[h + 1] - cut[h]), cols_of(p)]

        g2 = Gather4(s, view2, b, dev(ys[0], xs[0]), dev(ys[2], xs[2]))
        g2.begin()
        yield
        g2.relay()
        yield
        g2.wait_near()
        g2.wait_far()
        yield
        wide = ow_hbm.shape[1] // 2
        g1 = Gather4(
            s,
            lambda p, h: owg.at[:, rows_of(p), pl.ds(h * wide, wide)],
            a,
            dev(xs[0], ys[0]),
            dev(xs[2], ys[2]),
        )
        g1.begin()
        fw = []

        def forward(p):
            ref = owg.at[:, rows_of(p)]
            fw.append(s.go(ref, ref, partner))

        forward(a)
        yield
        g1.relay()
        yield
        g1.wait_near()
        forward(nxt(a, 1))
        forward(nxt(a, 3))
        yield
        g1.wait_far()
        forward(nxt(a, 2))
        yield
        for f in fw:
            f.wait_recv()

    def exchange(i):
        a, a_dev, b, b_dev = axes[i]
        own = kvbuf.at[i, a, z, core]
        cz = s.go(own, own, zpeer)

        def ring(zz):
            return Gather4(
                s,
                lambda slot, h: kvbuf.at[i, slot, zz, core, pl.ds(h * half, half)],
                a,
                a_dev[0],
                a_dev[2],
            )

        gk, go = ring(z), ring(1 - z)
        gq = Gather4(
            s, lambda slot, h: qbuf.at[i, slot, pl.ds(h * half, half)], b, b_dev[0], b_dev[2]
        )
        gk.begin()
        gq.begin()
        fw = []

        def forward(p, zz):
            ref = kvbuf.at[i, p, zz, core]
            fw.append(s.go(ref, ref, partner))

        forward(a, z)
        yield
        gk.relay()
        gq.relay()
        yield
        cz.wait_recv()
        go.begin()
        forward(a, 1 - z)
        yield
        gk.wait_near()
        forward(nxt(a, 1), z)
        forward(nxt(a, 3), z)
        yield
        gk.wait_far()
        forward(nxt(a, 2), z)
        go.relay()
        yield
        go.wait_near()
        forward(nxt(a, 1), 1 - z)
        forward(nxt(a, 3), 1 - z)
        yield
        go.wait_far()
        forward(nxt(a, 2), 1 - z)
        gq.wait_near()
        gq.wait_far()
        yield
        for f in fw:
            f.wait_recv()

    def project(i):
        a, _, b, _ = axes[i]
        values = jnp.concatenate([full[p, i] for p in range(NT)], axis=1).astype(F32)
        hidden = normalize(values)[0].astype(BF)
        qbuf[i, b] = jnp.dot(hidden, wq[...], preferred_element_type=F32).astype(BF)
        keys = wk.shape[1]
        kvbuf[i, a, z, core, :, 0:keys] = jnp.dot(
            hidden, wk[...], preferred_element_type=F32
        ).astype(BF)
        kvbuf[i, a, z, core, :, keys:] = jnp.dot(
            hidden, wv[...], preferred_element_type=F32
        ).astype(BF)

    def term(p):
        acc = jnp.zeros((rows, width), F32)
        for j in range(3):
            acc = acc + lax.dot_general(
                cots[j],
                cw[j, p * width : (p + 1) * width],
                (((1,), (1,)), ((), ())),
                preferred_element_type=F32,
            )
        terms_ref[p] = acc.astype(BF)

    keys = NX * NZ * NC * count
    lane2 = lax.broadcasted_iota(jnp.int32, (2 * count, 128), 1)
    lane = lax.broadcasted_iota(jnp.int32, (count, 128), 1)

    def attend(i, ks):
        b = axes[i][2]
        r0, r1 = nxt(b, ks[0]), nxt(b, ks[1])
        q = jnp.concatenate([qbuf[i, r0], qbuf[i, r1]], axis=0)
        q = (q.astype(F32) * KEY ** (-0.5)).astype(BF)
        k = kvbuf[i, :, :, :, :, 0:128].reshape(keys, 128)
        parts = []
        stats = jnp.zeros((2 * count, 128), F32)
        for h in range(2):
            qh = jnp.where((lane2 < KEY) if h == 0 else (lane2 >= KEY), q, jnp.zeros_like(q))
            sc = lax.dot_general(qh, k, (((1,), (1,)), ((), ())), preferred_element_type=F32)
            top = jnp.max(sc, axis=-1, keepdims=True)
            w = jnp.exp(sc - top)
            total = jnp.sum(w, axis=-1, keepdims=True)
            v = kvbuf[i, :, :, :, :, 128 + 128 * h : 384 + 128 * h].reshape(keys, 256)
            acc = jnp.dot(w.astype(BF), v, preferred_element_type=F32) / total
            parts.append(acc)
            stats = jnp.where(lane2 == h, top + jnp.log(total), stats)
        mid = jnp.where(lane2 < 64, parts[0][:, 128:], parts[1][:, :128])
        for n, r in enumerate((r0, r1)):
            at = slice(n * count, (n + 1) * count)
            obuf[i, r, :, 0:128] = parts[0][at, :128].astype(BF)
            obuf[i, r, :, 128:256] = mid[at].astype(BF)
            obuf[i, r, :, 256:384] = parts[1][at, 128:].astype(BF)
            lbuf[i, r] = stats[at].T[0:8]

    osent = [[], []]

    def send_out(i, k):
        b, b_dev = axes[i][2], axes[i][3]
        dev = b_dev[k - 1]
        osent[i].append(s.go(obuf.at[i, nxt(b, k)], orecv.at[i, b], dev))
        osent[i].append(s.go(lbuf.at[i, nxt(b, k)], lrecv.at[i, b], dev))

    def combine(i):
        b = axes[i][2]
        orecv[i, b] = obuf[i, b]
        lrecv[i, b] = lbuf[i, b]
        for c in osent[i]:
            c.wait_recv()
        logs = []
        for r in range(4):
            wide = jnp.concatenate([lrecv[i, r], jnp.zeros((120, 128), F32)], axis=0).T
            logs.append([wide[:, h : h + 1] for h in range(2)])
        wts = []
        for h in range(2):
            top = logs[0][h]
            for r in range(1, 4):
                top = jnp.maximum(top, logs[r][h])
            e = [jnp.exp(logs[r][h] - top) for r in range(4)]
            total = e[0] + e[1] + e[2] + e[3]
            wts.append([er / total for er in e])
        for g in range(3):
            acc = jnp.zeros((count, 128), F32)
            for r in range(4):
                if g == 0:
                    w = wts[0][r]
                elif g == 2:
                    w = wts[1][r]
                else:
                    w = jnp.where(lane < 64, wts[0][r], wts[1][r])
                acc = acc + orecv[i, r, :, 128 * g : 128 * g + 128].astype(F32) * w
            att[t, i, :, 128 * g : 128 * g + 128] = acc.astype(BF)
        ring = Gather4(
            s, lambda slot, h: att.at[slot, i, pl.ds(h * half, half)], t, plus, minus
        )
        ring.begin()
        return ring

    def step(gen):
        next(gen, None)

    tok0, tok1 = token_ring(0), token_ring(1)
    tok0.begin()
    up = s.go(cot_hbm.at[:, count - edge : count], cotx.at[:, 0:edge], seq_next(1))
    down = s.go(cot_hbm.at[:, 0:edge], cotx.at[:, edge + count : 2 * edge + count], seq_prev())
    lcot.wait()
    up.wait_recv()
    down.wait_recv()

    @pl.when(me == 0)
    def _():
        cotx[:, 0:edge] = jnp.zeros((2, edge, width), BF)

    @pl.when(me == last)
    def _():
        cotx[:, edge + count : 2 * edge + count] = jnp.zeros((2, edge, width), BF)

    for j in range(3):
        cots[j] = cotx[:, (2 - j) * edge : (2 - j) * edge + count].reshape(rows, width)
    lcw.wait()
    term(0)
    tok0.relay()
    weights = weight_gather()
    step(weights)
    tok1.begin()
    for p in range(1, NT):
        term(p)
    ltok.wait()
    for c in lws:
        c.wait()
    step(weights)
    tok0.wait_near()
    tok0.wait_far()
    tok1.relay()
    project(0)
    ex0 = exchange(0)
    step(ex0)
    step(weights)
    step(weights)
    step(weights)
    step(ex0)
    step(ex0)
    tok1.wait_near()
    tok1.wait_far()
    project(1)
    ex1 = exchange(1)
    step(ex1)
    step(weights)
    step(ex0)
    step(ex1)
    step(ex0)
    step(ex1)
    step(ex0)
    step(weights)
    step(ex0)
    step(ex1)
    step(weights)
    step(ex0)
    attend(0, (2, 1))
    send_out(0, 2)
    send_out(0, 1)
    step(ex1)
    step(weights)
    attend(0, (3, 0))
    send_out(0, 3)
    step(ex1)
    step(ex1)
    step(ex1)
    attend(1, (2, 1))
    send_out(1, 2)
    send_out(1, 1)
    ring0 = combine(0)
    attend(1, (3, 0))
    send_out(1, 3)
    ring0.relay()
    ring1 = combine(1)
    ring1.relay()
    ring0.wait_near()
    ring0.wait_far()
    ring1.wait_near()
    ring1.wait_far()
    for gen in (ex0, ex1, weights):
        for _ in gen:
            pass
    s.drain()


def in_hbm(v):
    return pltpu.with_memory_space_constraint(v, pltpu.HBM)


def front(tokens, cot, wq, wk, wv, ow, cw):
    seqs, count, width = tokens.shape
    keys, vals = wk.shape[1], wv.shape[1]
    n = 12 + 2 + 3 + 16 + 2 * 27 + 12 + 12
    return pl.pallas_call(
        front_kernel,
        name="front",
        out_shape=(
            jax.ShapeDtypeStruct((NT, seqs, count, vals), BF),
            jax.ShapeDtypeStruct((NT, seqs, count, width), BF),
            jax.ShapeDtypeStruct((seqs, count + 2 * CONV_DILATION, width), BF),
            jax.ShapeDtypeStruct((NT, seqs * count, width), BF),
            jax.ShapeDtypeStruct((NT - 1,) + ow.shape, BF),
        ),
        in_specs=[HSPEC] * 7,
        out_specs=(VSPEC,) * 5,
        scratch_shapes=[
            VMEM(wq.shape, BF),
            VMEM(wk.shape, BF),
            VMEM(wv.shape, BF),
            VMEM(cw.shape, BF),
            VMEM((3, seqs * count, width), BF),
            VMEM((seqs, 4, count, keys), BF),
            VMEM((seqs, 4, NZ, NC, count, keys + vals), BF),
            VMEM((seqs, 4, count, vals), BF),
            VMEM((seqs, 4, count, vals), BF),
            VMEM((seqs, 4, 8, count), F32),
            VMEM((seqs, 4, 8, count), F32),
            pltpu.SemaphoreType.DMA((n,)),
            pltpu.SemaphoreType.DMA((n,)),
            pltpu.SemaphoreType.DMA((6,)),
        ],
        compiler_params=params(1, 28),
    )(*[in_hbm(v) for v in (tokens, cot, wq, wk, wv, ow, cw)])


def tail_kernel(
    att, full, cotx, terms, ow, owg, cw,
    block_out, out_ref, residual,
    ug_ref, rt, blk, units, cots, taps, halo, st,
    send, recv, sums, r1, mid, r2, fin, zrecv, ss, rs,
):
    x, y, z, core = seq_pos()
    t, plus, minus = tensor_ring()
    me = lax.axis_index("seq")
    last = NX * NY * NZ * NC - 1
    rows, local = terms.shape[1:]
    half = rows // 2
    width = NT * local
    edge = CONV_DILATION
    total = 3 * width
    mine = total // 2
    tile = 256
    tiles = mine // tile
    per_tap = width // tile

    def pick(u, v):
        return jnp.where(core == 0, u, v)

    def along_x(k):
        return seq_dev(nxt(x, k), y, z, core)

    def along_y(k):
        return seq_dev(x, nxt(y, k), z, core)

    xr = (x, {"seq": along_x(1)}, {"seq": along_x(3)})
    yr = (y, {"seq": along_y(1)}, {"seq": along_y(3)})
    xy = (
        (pick(x, y), *({"seq": pick(along_x(k), along_y(k))} for k in (1, 3))),
        (pick(y, x), *({"seq": pick(along_y(k), along_x(k))} for k in (1, 3))),
    )
    axis_order = ((xr, yr), (yr, xr), xy)
    partner = {"seq": seq_dev(x, y, z, 1 - core)}
    zpeer = {"seq": seq_dev(x, y, 1 - z, core)}
    opposite = {"tensor": nxt(t, 2)}
    after, before = seq_next(1), seq_prev()
    greet([plus, minus, opposite, partner, zpeer, *xr[1:], *yr[1:], after, before])

    s = Sender(ss, rs)
    s.n = tiles

    red = Reduce4(
        s,
        lambda p, h: terms.at[p, pl.ds(h * half, half)],
        lambda i, h: rt.at[i],
        t,
        plus,
        minus,
    )
    red.begin()
    for j in range(3):
        cots[j] = cotx[:, (2 - j) * edge : (2 - j) * edge + half].reshape(rows, local)
    averages, invs = [], []
    for h in range(2):
        at = slice(h * half, (h + 1) * half)
        mixed = jnp.dot(att[t, h], ow[...], preferred_element_type=F32)
        for k in range(1, NT):
            mixed = mixed + jnp.dot(att[nxt(t, k), h], owg[k - 1], preferred_element_type=F32)
        for p in range(NT):
            blk[p, at] = (
                mixed[:, p * local : (p + 1) * local] + full[p, h].astype(F32)
            ).astype(BF)
        values = jnp.concatenate([blk[i, at] for i in range(NT)], axis=1).astype(F32)
        average = jnp.mean(values, axis=-1, keepdims=True)
        centred = values - average
        inv = lax.rsqrt(jnp.mean(centred * centred, axis=-1, keepdims=True) + eps_norm)
        units[at] = gelu_exact(centred * inv).astype(BF)
        averages.append(average)
        invs.append(inv)
    red.combine()

    def product(q):
        tap = lax.div(q, per_tap)
        col = pl.multiple_of(lax.rem(q, per_tap) * tile, tile)
        return lax.dot_general(
            units[:, pl.ds(col, tile)],
            cots[tap],
            (((0,), (0,)), ((), ())),
            preferred_element_type=F32,
        )

    def exchange(i):
        return pltpu.make_async_remote_copy(
            src_ref=send.at[i],
            dst_ref=recv.at[i],
            send_sem=ss.at[i],
            recv_sem=rs.at[i],
            device_id=partner,
            device_id_type=MESH,
        )

    @pl.loop(0, tiles)
    def _(i):
        send[i] = product((1 - core) * tiles + i).astype(BF)
        exchange(i).start()

    @pl.loop(0, tiles)
    def _(i):
        own = product(core * tiles + i)
        exchange(i).wait_recv()
        row = pl.multiple_of(i * tile, tile)
        both = (own + recv[i].astype(F32)).astype(BF)
        for w in range(3):
            sums[w, pl.ds(row, tile)] = both[:, w * 128 : (w + 1) * 128]

    big = mine // 4
    small = big // 4
    bh = (0, big // 2)
    bn = (big // 2, big // 2)
    cut = (small // 2 + 15) // 16 * 16
    sh = (0, cut)
    sn = (cut, small - cut)
    scale = (rows * NX * NY * NZ * NC) ** (-0.5)

    def m16(v):
        return pl.multiple_of(v, 16)

    def wave(w):
        (a, ap, am), (b, bp, bm) = axis_order[w]
        base = core * mine
        first = Reduce4(
            s,
            lambda p, h: sums.at[w, pl.ds(m16(p * big + bh[h]), bn[h])],
            lambda i, h: r1.at[w, i],
            a,
            ap,
            am,
        )
        first.begin()
        yield
        first.combine()
        yield
        h0, h1 = first.finish()
        mid[w, 0 : big // 2] = h0.astype(BF)
        mid[w, big // 2 : big] = h1.astype(BF)
        second = Reduce4(
            s,
            lambda p, h: mid.at[w, pl.ds(m16(p * small + sh[h]), sn[h])],
            lambda i, h: r2.at[w, i, pl.ds(0, sn[h])],
            b,
            bp,
            bm,
        )
        second.begin()
        yield
        second.combine()
        yield
        h0, h1 = second.finish()
        fin[w, 0:cut] = h0.astype(BF)
        fin[w, cut:small] = h1.astype(BF)
        cz = s.go(fin.at[w], zrecv.at[w], zpeer)
        yield
        cz.wait_recv()
        out_ref[w, pl.ds(m16(base + a * big + b * small), small)] = (
            (fin[w].astype(F32) + zrecv[w].astype(F32)) * scale
        ).astype(BF)
        g2 = Gather4(
            s,
            lambda p, h: out_ref.at[w, pl.ds(m16(base + a * big + p * small + sh[h]), sn[h])],
            b,
            bp,
            bm,
        )
        g2.begin()
        yield
        g2.relay()
        yield
        g2.wait_near()
        g2.wait_far()
        g1 = Gather4(
            s,
            lambda p, h: out_ref.at[w, pl.ds(m16(base + p * big + bh[h]), bn[h])],
            a,
            ap,
            am,
        )
        g1.begin()
        fw = []

        def forward(p):
            ref = out_ref.at[w, pl.ds(m16(base + p * big), big)]
            fw.append(s.go(ref, ref, partner))

        forward(a)
        yield
        g1.relay()
        yield
        g1.wait_near()
        forward(nxt(a, 1))
        forward(nxt(a, 3))
        yield
        g1.wait_far()
        forward(nxt(a, 2))
        yield
        for f in fw:
            f.wait_recv()

    runs = [wave(w) for w in range(3)]

    def advance():
        for run in runs:
            next(run, None)

    advance()


    def tap(j):
        return jnp.dot(units[...], cw[j], preferred_element_type=F32).reshape(2, half, local)

    taps[0] = tap(0)
    up = s.go(taps.at[0, :, half - edge : half], halo.at[0], after)
    taps[2] = tap(2)
    down = s.go(taps.at[2, :, 0:edge], halo.at[1], before)
    advance()
    taps[1] = tap(1)
    advance()
    parts = red.finish()
    for h in range(2):
        ug_ref[h * half : (h + 1) * half] = parts[h]
    lane = lax.broadcasted_iota(jnp.int32, (half, 128), 1)
    for h in range(2):
        at = pl.ds(h * half, half)
        n = (blk[t, at].astype(F32) - averages[h]) * invs[h]
        slope = ug_ref[h * half : (h + 1) * half] * gelu_slope(n)
        one = jnp.sum(slope, axis=-1, keepdims=True)
        two = jnp.sum(slope * n, axis=-1, keepdims=True)
        stats = jnp.where(lane == 0, one, jnp.where(lane == 1, two, 0.0))
        st[t, h] = stats.T[0:8]
    stat_copies = [s.go(st.at[t], st.at[t], d) for d in (plus, minus, opposite)]
    advance()
    up.wait_recv()
    down.wait_recv()
    for h in range(2):
        own = blk[t, pl.ds(h * half, half)].astype(F32) + taps[1, h]
        left = jnp.where(me == 0, 0.0, halo[0, h])
        right = jnp.where(me == last, 0.0, halo[1, h])
        block_out[h, 0:edge] = (own[:edge] + left + taps[2, h, edge:half]).astype(BF)
        block_out[h, edge:half] = (own[edge:] + taps[0, h, 0 : half - edge] + right).astype(BF)

    advance()
    advance()
    for c in stat_copies:
        c.wait_recv()
    for h in range(2):
        at = pl.ds(h * half, half)
        n = (blk[t, at].astype(F32) - averages[h]) * invs[h]
        slope = ug_ref[h * half : (h + 1) * half] * gelu_slope(n)
        both = (st[0, h] + st[1, h] + st[2, h] + st[3, h]) * (1.0 / width)
        wide = jnp.concatenate([both, jnp.zeros((120, 128), F32)], axis=0).T
        grad = (slope - wide[:, 0:1] - n * wide[:, 1:2]) * invs[h]
        residual[h] = (cotx[h, edge : edge + half].astype(F32) + grad).astype(BF)
    for _ in range(7):
        advance()
    s.drain()

    @pl.loop(0, tiles)
    def _(i):
        exchange(i).wait_send()


def tail(attended, full, cotx, terms, out_weight, others, conv_weight):
    _, rows, local = terms.shape
    width = local * NT
    half = rows // 2
    edge = CONV_DILATION
    mine = 3 * width // 2
    big, small = mine // 4, mine // 16
    cut = (small // 2 + 15) // 16 * 16
    n = mine // 256 + 6 + 3 * (6 * 4 + 1 + 4) + 2 + 3
    return pl.pallas_call(
        tail_kernel,
        name="tail",
        out_shape=(
            jax.ShapeDtypeStruct((2, half, local), BF),
            jax.ShapeDtypeStruct((local // 128, 3 * width, 128), BF),
            jax.ShapeDtypeStruct((2, half, local), BF),
        ),
        in_specs=[VSPEC] * 7,
        out_specs=(VSPEC,) * 3,
        scratch_shapes=[
            VMEM((rows, local), F32),
            VMEM((8, half, local), BF),
            VMEM((NT, rows, local), BF),
            VMEM((rows, width), BF),
            VMEM((3, rows, local), BF),
            VMEM((3, 2, half, local), F32),
            VMEM((2, 2, edge, local), F32),
            VMEM((NT, 2, 8, 128), F32),
            VMEM((mine // 256, 256, local), BF),
            VMEM((mine // 256, 256, local), BF),
            VMEM((3, mine, 128), BF),
            VMEM((3, 8, big // 2, 128), BF),
            VMEM((3, big, 128), BF),
            VMEM((3, 8, cut, 128), BF),
            VMEM((3, small, 128), BF),
            VMEM((3, small, 128), BF),
            pltpu.SemaphoreType.DMA((n,)),
            pltpu.SemaphoreType.DMA((n,)),
        ],
        compiler_params=params(3, 24),
    )(attended, full, cotx, terms, out_weight, others, conv_weight)


def side_by_side_kernel(parts, out):
    for w in range(parts.shape[0]):
        out[:, w * 128 : (w + 1) * 128] = parts[w]


def side_by_side(parts):
    n, rows, cols = parts.shape
    step = rows // 6
    return pl.pallas_call(
        side_by_side_kernel,
        name="side_by_side",
        grid=(6,),
        out_shape=jax.ShapeDtypeStruct((rows, n * cols), BF),
        in_specs=[pl.BlockSpec((n, step, cols), lambda i: (0, i, 0))],
        out_specs=pl.BlockSpec((step, n * cols), lambda i: (i, 0)),
        compiler_params=pltpu.CompilerParams(vmem_limit_bytes=8 * 1024 * 1024),
    )(parts)


def body(tokens_in, query_weight, key_weight, value_weight, out_weight, conv_weight, cotangent):
    local = tokens_in.shape[2]
    attended, full, cotx, terms, others = front(
        tokens_in, cotangent, query_weight, key_weight, value_weight, out_weight, conv_weight
    )
    block_out, conv_grad, residual_grad = tail(
        attended, full, cotx, terms, out_weight, others, conv_weight
    )
    conv_grad = side_by_side(conv_grad).reshape(3, local * NT, local)
    return (block_out, conv_grad, residual_grad)


def solution(mesh):
    placed = (
        P(None, "seq", "tensor"),
        P(None, "tensor"),
        P(None, "tensor"),
        P(None, "tensor"),
        P("tensor", None),
        P(None, None, "tensor"),
        P(None, "seq", "tensor"),
    )
    return jax.shard_map(
        body,
        mesh=mesh,
        in_specs=placed,
        out_specs=(P(None, "seq", "tensor"), P(None, None, "tensor"), P(None, "seq", "tensor")),
        check_vma=False,
    )
```
